256 devices in a mesh: seq: 64 (over z, x, core), head: 4 (over y).
Axes of the slice: x: 4, y: 4, z: 8, core: 2. Of those that a mesh axis runs over, the one named last changes fastest.
Arguments:
- queries: bfloat16 [8192, 2048], P('seq', 'head'), may hold values from -200 to 200
- keys: bfloat16 [8192, 2048], P('seq', 'head'), may hold values from -6 to 6
- values: bfloat16 [8192, 2048], P('seq', 'head'), may hold values from -6 to 6
- bucket: int32 [8192, 1], replicated, may hold values from 0 to 63; in each aligned block of 128 rows (0 to 127, 128 to 255, ...) at most 3 rows name the same one
- w_out: bfloat16 [2048, 4096], P('head'), may hold values from -0.125 to 0.125
- grad_out: bfloat16 [8192, 4096], P('seq'), may hold values from -16 to 16
Outputs:
- layer_out: bfloat16 [8192, 4096], P('seq', 'head')
- grad_queries: bfloat16 [8192, 2048], P('seq', 'head')
- grad_keys: bfloat16 [8192, 2048], P('seq', 'head')
- grad_values: bfloat16 [8192, 2048], P('seq', 'head')
- grad_weight: float32 [2048, 4096], P('head', 'seq')
The draws below stay inside these ranges and needn't reach their ends.
Inputs may be any that keep to these rules, and one draw needn't show every extreme that they name: Bucket b belongs to the b-th index of seq; buckets b and b-1 are neighbouring tree leaves. Among the tokens of one block of 128 at most 3 share a bucket, and exactly 3 do in some block.
All inputs are finite; a program needn't handle non-finite values.
Results may differ from the reference program's by a relative error of at most 0.012.
Values may be sent and summed in bfloat16 or wider, within the bound.
No kernel may reach another device: no remote copies, remote signals or barrier semaphores. Data moves between devices by JAX's collectives and lax.ppermute only.
A program may use at most 128 MiB of HBM per device.

```python
import math
import jax
import jax.numpy as jnp
import numpy as np
from jax import lax

D = 4096
HEADS = 16
HSZ = 128
TOK_DEV = 128
TOKENS = 8192
HD = 2048
CAP = 3
N_SEQ = 64


def query_key(key):
    base = jax.random.fold_in(key, 7)
    first, second = jax.random.split(base, 2)
    shape = (TOKENS, HD)
    keys_part = jnp.clip(jax.random.normal(first, shape, jnp.float32), -6.0, 6.0)
    queries_part = jnp.clip(jax.random.normal(second, shape, jnp.float32), -6.0, 6.0)
    return (queries_part, keys_part)


def draw_queries(key, part):
    return query_key(key)[0].astype(jnp.bfloat16)


def draw_keys(key, part):
    return query_key(key)[1].astype(jnp.bfloat16)


def raised(result, own_key, source, target, blocks, factor):
    def block_of(dim):
        return (jnp.arange(result.shape[dim]) // (result.shape[dim] // blocks)).reshape((-1,) + (1,) * (result.ndim - 1 - dim))

    first = jax.random.permutation(own_key, blocks)[block_of(target)]
    other_side = (block_of(target) + blocks // 2) % blocks
    return jnp.where((block_of(source) == first) | (block_of(source) == other_side), factor * result, result)


def steps_of(stream_key, shape, pieces, least, high):
    def one(position, shards_of):
        heights = jax.random.uniform(jax.random.fold_in(jax.random.fold_in(stream_key, 6), position), (shards_of,), jnp.float32, least / len(pieces), high / len(pieces))
        return jnp.repeat(jnp.exp(heights), shape[position] // shards_of).reshape((-1,) + (1,) * (len(shape) - position - 1))

    level = one(*pieces[0])
    for cut in pieces[1:]:
        level = level * one(*cut)
    return level


def assign_block(stream_key, own, number, rows, count, top, bound, lean):
    order = jax.random.permutation(stream_key, count)
    heavy_load, ordinary = shares(count, rows * top, bound, lean, True), shares(count, rows * top, bound, lean, False)
    places = jnp.arange(count)

    def named(lengths, turn):
        used = int((lengths > 0).sum())
        fixed = max(1, used // 4)
        passed = fixed + (places - fixed + turn * (used - fixed)) % max(1, count - fixed)
        return jnp.zeros((count,), jnp.int32).at[order[jnp.where(places < fixed, places, passed)]].set(jnp.asarray(lengths, jnp.int32))

    lengths = jnp.where(number % 4 == 0, named(heavy_load, number // 4), named(ordinary, number - number // 4 - 1))
    mixed = jax.random.permutation(jax.random.fold_in(own, 3), count)
    giver, sink = mixed[0:count // 2 * 2:2], mixed[1:count // 2 * 2:2]
    slack = jnp.minimum(lengths[giver] - 1, bound - lengths[sink]) // 2
    slack = jnp.where((giver == order[0]) | (sink == order[0]) | (lengths[sink] == 0), 0, jnp.maximum(slack, 0))
    passed = jax.random.randint(jax.random.fold_in(own, 4), (count // 2,), 0, 1 << 20) % (slack + 1)
    lengths = lengths.at[giver].add(-passed).at[sink].add(passed)
    members = jnp.searchsorted(jnp.cumsum(lengths), jnp.arange(rows * top), side="right").astype(jnp.int32)
    table = members.reshape(top, rows).T
    table = table[jax.random.permutation(jax.random.fold_in(own, 1), rows)]
    turn = jax.random.randint(jax.random.fold_in(own, 2), (rows, 1), 0, top)
    return jnp.take_along_axis(table, (jnp.arange(top)[None, :] + turn) % top, axis=1)


def shares(number_of, total, bound, skew, full):
    weights = [(1 << 20) // math.isqrt(rank ** skew) + 1 for rank in range(1, number_of + 1)]
    largest = bound if full else min(bound, max(-(-total // number_of), total * weights[0] // sum(weights)))
    least = 1 if total - largest >= number_of - 1 else 0
    holding, spare = [largest] + [least] * (number_of - 1), total - largest - least * (number_of - 1)
    while spare > 0:
        movable = [i for i in range(1, number_of) if holding[i] < largest] or [i for i in range(1, number_of) if holding[i] < bound]
        whole, remaining = sum([weights[i] for i in movable]), spare
        for i in movable:
            extra = min(bound - holding[i], max(1, remaining * weights[i] // whole), spare)
            holding[i] = holding[i] + extra
            spare = spare - extra
    return np.array(holding)


def centred(key, shape, deviation, reach, cuts=(), kind=jnp.bfloat16):
    gain = steps_of(key, shape, cuts, -0.22, 0.18) if cuts else 1.0
    entries = jax.random.normal(key, shape, jnp.float32) * deviation * gain
    return jnp.minimum(jnp.maximum(entries, -reach), reach).astype(kind)


def gaussian_with(rng, dims, spread, bound, shards, heavy, held_as=jnp.bfloat16):
    drawn = spread * jax.random.normal(rng, dims, jnp.float32)
    if shards:
        drawn = drawn * steps_of(rng, dims, shards, -0.22, 0.18)
    return jnp.clip(raised(drawn, jax.random.fold_in(rng, 3), *heavy), -bound, bound).astype(held_as)


def setup_inputs(seed: int = 0) -> dict:
    streams_of = jax.random.split(jax.random.key(seed), 7)
    queries = draw_queries(jax.random.fold_in(streams_of[6], 71), 0)
    keys = draw_keys(jax.random.fold_in(streams_of[6], 71), 0)
    values = centred(streams_of[2], (TOKENS, HD), 1.0, 6.0, ((0, 64), (1, 4)))
    bucket_keys = jax.random.split(jax.random.fold_in(streams_of[3], 1), TOKENS // TOK_DEV)
    bucket_turns = jax.random.permutation(jax.random.fold_in(streams_of[3], 3), TOKENS // TOK_DEV)
    bucket = jax.vmap(lambda own, number: assign_block(jax.random.fold_in(streams_of[3], 2), own, number, TOK_DEV, N_SEQ, 1, CAP, 2))(bucket_keys, bucket_turns).reshape((TOKENS, 1))
    w_out = centred(streams_of[4], (HD, D), HD ** -0.5, 0.125, ((0, 4),))
    grad_out = gaussian_with(streams_of[5], (TOKENS, D), 1.0, 16.0, ((0, 64),), (0, 1, 64, 4.0))
    return dict(queries=queries, keys=keys, values=values, bucket=bucket, w_out=w_out, grad_out=grad_out)


def member_table(bucket_grid, owner, slot_count):
    matches = (bucket_grid == owner).astype(jnp.int32)
    ranking = jnp.cumsum(matches, axis=1) - matches
    slot_ids = jnp.arange(slot_count, dtype=jnp.int32)
    placed = matches[:, :, None] * (ranking[:, :, None] == slot_ids[None, None, :]).astype(jnp.int32)
    sources = bucket_grid.shape[0]
    stride = bucket_grid.shape[1]
    offsets = jnp.arange(sources, dtype=jnp.int32)[:, None] * stride + jnp.arange(stride, dtype=jnp.int32)[None, :]
    where_at = lax.optimization_barrier(jnp.sum(placed * offsets[:, :, None], axis=1)).reshape(-1)
    present = lax.optimization_barrier(jnp.sum(placed, axis=1)).reshape(-1)
    return (where_at, present)

def allowed_mask(where_here, alive_here, where_before, alive_before):
    amount = where_here.shape[0]
    asking = alive_here[:, None] > 0
    inside = (where_here[None, :] <= where_here[:, None]) & (alive_here[None, :] > 0) & asking
    inside = inside | (jnp.arange(amount)[:, None] == jnp.arange(amount)[None, :])
    earlier = (where_before[None, :] <= where_here[:, None]) & (alive_before[None, :] > 0) & asking
    return jnp.concatenate([inside, earlier], axis=1)

def softmax_rows(scores, allowed):
    masked = jnp.where(allowed[None], scores, -1e+30)
    largest = lax.optimization_barrier(jnp.max(masked, axis=2, keepdims=True))
    weights = jnp.where(allowed[None], jnp.exp(masked - largest), 0.0)
    return weights / lax.optimization_barrier(jnp.sum(weights, axis=2, keepdims=True))

def reference(queries, keys, values, bucket, w_out, grad_out):
    scaling = 1.0 / math.sqrt(HSZ)
    bucket_grid = bucket[:, 0].reshape(N_SEQ, TOK_DEV)
    grad_heads = jnp.dot(grad_out, w_out.T, preferred_element_type=jnp.float32).astype(jnp.bfloat16)

    def gather_rows(source, where_at, present):
        return jnp.take(source, where_at, axis=0) * present[:, None].astype(source.dtype)

    def split_heads(block):
        return block.astype(jnp.float32).reshape(block.shape[0], HEADS, HSZ)

    def flatten(block):
        return block.reshape(block.shape[0], HEADS * HSZ)

    def bucket_pass(owner):
        where_here, alive_here = member_table(bucket_grid, owner, CAP)
        where_before, alive_before = member_table(bucket_grid, owner - 1, CAP)
        allowed = allowed_mask(where_here, alive_here, where_before, alive_before)
        query_rows = split_heads(gather_rows(queries, where_here, alive_here))
        key_all = split_heads(jnp.concatenate([gather_rows(keys, where_here, alive_here), gather_rows(keys, where_before, alive_before)], axis=0))
        value_all = split_heads(jnp.concatenate([gather_rows(values, where_here, alive_here), gather_rows(values, where_before, alive_before)], axis=0))
        grad_rows = split_heads(gather_rows(grad_heads, where_here, alive_here))
        scores = jnp.einsum('qhd,khd->hqk', query_rows, key_all) * scaling
        probs = softmax_rows(scores, allowed)
        rounded = lax.optimization_barrier(probs.astype(jnp.bfloat16)).astype(jnp.float32)
        attended = jnp.einsum('hqk,khd->qhd', rounded, value_all).astype(jnp.bfloat16)
        centre = lax.optimization_barrier(jnp.sum(attended.astype(jnp.float32) * grad_rows, axis=2))
        dprobs = jnp.einsum('qhd,khd->hqk', grad_rows, value_all)
        dscores = probs * (dprobs - jnp.transpose(centre)[:, :, None])
        dround = lax.optimization_barrier(dscores.astype(jnp.bfloat16)).astype(jnp.float32)
        grad_query = (jnp.einsum('hqk,khd->qhd', dround, key_all) * scaling).astype(jnp.bfloat16)
        grad_key = jnp.einsum('hqk,qhd->khd', dround, query_rows) * scaling
        grad_value = jnp.einsum('hqk,qhd->khd', rounded, grad_rows)
        slot_total = where_here.shape[0]
        return (flatten(attended), flatten(grad_query), flatten(grad_key[:slot_total]), flatten(grad_value[:slot_total]), flatten(grad_key[slot_total:]).astype(jnp.bfloat16), flatten(grad_value[slot_total:]).astype(jnp.bfloat16))
    outcome = lax.map(bucket_pass, jnp.arange(N_SEQ, dtype=jnp.int32))
    attended_all, query_all, key_own, value_own, key_prev, value_prev = outcome
    nothing = jnp.zeros_like(key_prev[:1])
    key_next = jnp.concatenate([key_prev[1:], nothing], axis=0)
    value_next = jnp.concatenate([value_prev[1:], nothing], axis=0)
    key_total = (key_own + key_next.astype(jnp.float32)).astype(jnp.bfloat16)
    value_total = (value_own + value_next.astype(jnp.float32)).astype(jnp.bfloat16)
    owners = jnp.arange(N_SEQ, dtype=jnp.int32)
    onehot = (bucket_grid[:, :, None] == owners[None, None, :]).astype(jnp.int32)
    ranking = lax.optimization_barrier(jnp.sum((jnp.cumsum(onehot, axis=1) - onehot) * onehot, axis=2))
    sources = jnp.arange(N_SEQ, dtype=jnp.int32)[:, None]
    lookup = (bucket_grid * (N_SEQ * CAP) + sources * CAP + ranking).reshape(-1).astype(jnp.int32)

    def collect(stacked):
        return jnp.take(stacked.reshape(-1, HEADS * HSZ), lookup, axis=0)
    attended_tok = collect(attended_all)
    layer_out = jnp.dot(attended_tok, w_out, preferred_element_type=jnp.float32).astype(jnp.bfloat16)
    grad_weight = jnp.dot(attended_tok.T, grad_out, preferred_element_type=jnp.float32)
    return (layer_out, collect(query_all), collect(key_total), collect(value_total), grad_weight)
```

```python
import functools
import math

import jax
import jax.numpy as jnp
from jax import lax
from jax.experimental import pallas as pl
from jax.experimental.pallas import tpu as pltpu
from jax.sharding import Mesh
from jax.sharding import PartitionSpec as P


HSZ = 128
SEQ = ("seq_0", "seq_1", "seq_2")


def shifted(value, axis, by):
    length = lax.axis_size(axis)
    return lax.ppermute(value, axis, [(i, (i + by) % length) for i in range(length)])


def passed_along(value, axis, by):
    length = lax.axis_size(axis)
    pairs = [(i, i + by) for i in range(length) if 0 <= i + by < length]
    return lax.ppermute(value, axis, pairs)


def member_table(bucket_grid, owner, slot_count):
    sources, stride = bucket_grid.shape
    matches = bucket_grid == owner
    token = jnp.arange(stride)
    earlier = (token[:, None] < token[None, :]).astype(jnp.bfloat16)
    ranking = jnp.dot(matches.astype(jnp.bfloat16), earlier, preferred_element_type=jnp.float32)
    offsets = (
        jnp.arange(sources, dtype=jnp.int32)[:, None] * stride
        + jnp.arange(stride, dtype=jnp.int32)[None, :]
    )
    where_at = []
    present = []
    for slot in range(slot_count):
        placed = (matches & (ranking == slot)).astype(jnp.int32)
        where_at.append(jnp.sum(placed * offsets, axis=1))
        present.append(jnp.sum(placed, axis=1))
    return (jnp.stack(where_at, axis=1).reshape(-1), jnp.stack(present, axis=1).reshape(-1))


NEVER = 1 << 30
NT = (((1,), (1,)), ((), ()))
TN = (((0,), (0,)), ((), ()))


def product(left, right, dims=(((1,), (0,)), ((), ()))):
    return lax.dot_general(left, right, dims, preferred_element_type=jnp.float32)


def hidden(query_at, key_at):
    slots = query_at.shape[0]
    seen = key_at <= query_at
    row = lax.broadcasted_iota(jnp.int32, (slots, 2 * slots), 0)
    column = lax.broadcasted_iota(jnp.int32, (slots, 2 * slots), 1)
    return jnp.where(seen | (row == column), 0.0, -1e30)


def probs_of(query, key_here, key_before, bias, scaling):
    slots = query.shape[0]
    here = product(query, key_here, NT) * scaling + bias[:, :slots]
    before = product(query, key_before, NT) * scaling + bias[:, slots:]
    largest = jnp.maximum(
        jnp.max(here, axis=1, keepdims=True), jnp.max(before, axis=1, keepdims=True)
    )
    here = jnp.exp(here - largest)
    before = jnp.exp(before - largest)
    total = jnp.sum(here, axis=1, keepdims=True) + jnp.sum(before, axis=1, keepdims=True)
    inverse = 1.0 / total
    return here * inverse, before * inverse


def bucket_kernel(
    scaling,
    slot_total,
    rows,
    prev,
    query_at,
    key_at,
    attended,
    grad_query,
    own_terms,
    prev_terms,
    held,
    spread,
):
    features = rows.shape[1] // 4
    heads = features // HSZ
    count, bands = attended.shape[0], attended.shape[1]
    tiles = spread.shape[0]
    bias = hidden(query_at[...], key_at[...])
    spread[...] = jnp.zeros(spread.shape, jnp.float32)
    for head in range(heads):
        def part(ref, index):
            return ref[:, index * features + head * HSZ : index * features + (head + 1) * HSZ]

        query, key, value, grad = (part(rows, index) for index in range(4))
        key_prev, value_prev = part(prev, 0), part(prev, 1)
        here, before = probs_of(query, key, key_prev, bias, scaling)
        here_b = here.astype(jnp.bfloat16)
        before_b = before.astype(jnp.bfloat16)
        out = product(here_b, value) + product(before_b, value_prev)
        held[...] = out
        for slot in range(slot_total):
            chunk = slot * heads + head
            spread[chunk % tiles, pl.ds(chunk // tiles, count, stride=bands), :] = held[
                pl.ds(slot, count, stride=slot_total), :
            ]
        out = out.astype(jnp.bfloat16).astype(jnp.float32)
        centre = jnp.sum(out * grad.astype(jnp.float32), axis=1, keepdims=True)
        d_here = (here * (product(grad, value, NT) - centre)).astype(jnp.bfloat16)
        d_before = (before * (product(grad, value_prev, NT) - centre)).astype(jnp.bfloat16)
        start, end = head * HSZ, (head + 1) * HSZ
        to_query = (product(d_here, key) + product(d_before, key_prev)) * scaling
        grad_query[:, start:end] = to_query.astype(jnp.bfloat16)
        own_terms[:, start:end] = product(d_here, query, TN) * scaling
        own_terms[:, features + start : features + end] = product(here_b, grad, TN)
        prev_terms[:, start:end] = (product(d_before, query, TN) * scaling).astype(jnp.bfloat16)
        prev_terms[:, features + start : features + end] = product(before_b, grad, TN).astype(
            jnp.bfloat16
        )
    for tile in range(tiles):
        attended[:, :, tile * HSZ : (tile + 1) * HSZ] = (
            spread[tile].reshape(count, bands, HSZ).astype(jnp.bfloat16)
        )


def weight_kernel(cols, depth, place, *refs):
    outs = refs[: 2 * cols]
    rows = refs[2 * cols : 3 * cols]
    kept = refs[3 * cols]
    sent = refs[3 * cols + 1 : 3 * cols + depth]
    total = refs[-1]
    columns = total.shape[1]
    step = 256
    for start in range(0, columns, step):
        acc = None
        for k in range(cols):
            for side in range(2):
                term = product(rows[k][side], outs[side * cols + k][:, start : start + step], TN)
                acc = term if acc is None else acc + term
        total[:, start : start + step] = acc
    width = columns // depth
    for k in range(depth):
        at = lax.rem(place[0] + k, depth)
        block = total[:, pl.ds(pl.multiple_of(at * width, width), width)]
        if k == 0:
            kept[...] = block
        else:
            sent[k - 1][...] = block.astype(jnp.bfloat16)


def home_kernel(slot_total, core, mine, returned, home, keep, give, spread):
    count, bands, lanes = returned.shape
    tokens, features = home.shape
    heads = features // HSZ
    tiles = lanes // HSZ
    used = min(tiles, slot_total * heads)
    for tile in range(used):
        block = returned[:, :, tile * HSZ : (tile + 1) * HSZ]
        spread[tile] = block.astype(jnp.float32).reshape(count * bands, HSZ)
    row = lax.broadcasted_iota(jnp.int32, (tokens, tokens), 0)
    column = lax.broadcasted_iota(jnp.int32, (tokens, tokens), 1)
    named = jnp.broadcast_to(mine[...], (tokens, tokens))
    across = named.T
    earlier = (named == across) & (column < row)
    ranking = jnp.sum(earlier.astype(jnp.int32), axis=1, keepdims=True)
    owner = lax.broadcasted_iota(jnp.int32, (tokens, count), 1)
    picks = []
    for slot in range(slot_total):
        match = (across[:, :count] == owner) & (ranking == slot)
        picks.append(jnp.where(match, 1.0, 0.0).astype(jnp.bfloat16))
    for head in range(heads):
        total = None
        for slot in range(slot_total):
            chunk = slot * heads + head
            rows = spread[chunk % tiles, pl.ds(chunk // tiles, count, stride=bands), :]
            term = product(picks[slot], rows.astype(jnp.bfloat16))
            total = term if total is None else total + term
        home[:, head * HSZ : (head + 1) * HSZ] = total.astype(jnp.bfloat16)
    half = features // 2
    keep[...] = home[:, pl.ds(pl.multiple_of(core[0] * half, HSZ), half)]
    give[...] = home[:, pl.ds(pl.multiple_of((1 - core[0]) * half, HSZ), half)]


def pack_kernel(slot_total, device, grid, queries, keys, values, out, weight, packed, total, spread):
    step = pl.program_id(0)
    term = product(out[...], weight[...], NT)

    @pl.when(step == 0)
    def _():
        total[...] = term

    @pl.when(step > 0)
    def _():
        total[...] += term

    @pl.when(step == pl.num_programs(0) - 1)
    def _():
        tokens, features = queries.shape
        count = packed.shape[0]
        bands = packed.shape[1]
        row = lax.broadcasted_iota(jnp.int32, (tokens, tokens), 0)
        column = lax.broadcasted_iota(jnp.int32, (tokens, tokens), 1)
        mine = grid[pl.ds(device[0], 1), :]
        named = jnp.broadcast_to(mine, (tokens, tokens))
        same = (named == named.T) & (row < column)
        ranking = jnp.sum(same.astype(jnp.int32), axis=0, keepdims=True)
        slot_of = ranking * count + mine
        slots = lax.broadcasted_iota(jnp.int32, (slot_total * count, tokens), 0)
        chosen = jnp.where(slots == slot_of, 1.0, 0.0).astype(jnp.bfloat16)
        arrays = (queries[...], keys[...], values[...], total[...].astype(jnp.bfloat16))
        tiles = spread.shape[0]
        for index in range(4):
            rows = product(chosen, arrays[index])
            for part in range(features // HSZ):
                for slot in range(slot_total):
                    chunk = (slot * 4 + index) * (features // HSZ) + part
                    spread[chunk % tiles, pl.ds(chunk // tiles, count, stride=bands), :] = rows[
                        slot * count : (slot + 1) * count, part * HSZ : (part + 1) * HSZ
                    ]
        for tile in range(tiles):
            packed[:, :, tile * HSZ : (tile + 1) * HSZ] = (
                spread[tile].reshape(count, bands, HSZ).astype(jnp.bfloat16)
            )


def slot_matrix(mine, slot_total, slots):
    token = jnp.arange(mine.shape[0])
    same = (mine[:, None] == mine[None, :]) & (token[None, :] < token[:, None])
    ranking = jnp.sum(same.astype(jnp.int32), axis=1)
    slot_of = mine * slot_total + ranking
    slot = jnp.arange(slots)[None, :]
    here = (slot == slot_of[:, None]).astype(jnp.bfloat16)
    return here


def picked(selection, rows):
    return jnp.dot(selection, rows, preferred_element_type=jnp.float32).astype(jnp.bfloat16)


def per_device(queries, keys, values, bucket, w_out, grad_out):
    sources = lax.axis_size(SEQ)
    device = lax.axis_index(SEQ)
    col = lax.axis_index("seq_1")
    core = lax.axis_index("seq_2")
    head = lax.axis_index("head")
    cols = lax.axis_size("seq_1")
    depth = lax.axis_size("seq_0")
    heads = lax.axis_size("head")
    token_rows, features = queries.shape
    model = grad_out.shape[1]
    groups = features // HSZ
    slot_total = max(2, 3 * token_rows // (2 * sources))
    slot_rows = sources * slot_total
    scaling = 1.0 / math.sqrt(HSZ)
    bucket_grid = bucket[:, 0].reshape(sources, token_rows)
    mine = lax.dynamic_index_in_dim(bucket_grid, device, 0, keepdims=False)
    back = slot_matrix(mine, slot_total, slot_rows)
    bands = 8
    split = 4
    whole = pl.BlockSpec((token_rows, features), lambda k: (0, 0))
    packed = pl.pallas_call(
        functools.partial(pack_kernel, slot_total),
        grid=(split,),
        in_specs=[
            pl.BlockSpec(memory_space=pltpu.SMEM),
            pl.BlockSpec((sources, token_rows), lambda k: (0, 0)),
            whole,
            whole,
            whole,
            pl.BlockSpec((token_rows, model // split), lambda k: (0, k)),
            pl.BlockSpec((features, model // split), lambda k: (0, k)),
        ],
        out_specs=pl.BlockSpec(
            (sources, bands, slot_total * 4 * features // bands), lambda k: (0, 0, 0)
        ),
        out_shape=jax.ShapeDtypeStruct(
            (sources, bands, slot_total * 4 * features // bands), jnp.bfloat16
        ),
        scratch_shapes=[
            pltpu.VMEM((token_rows, features), jnp.float32),
            pltpu.VMEM((slot_total * 4 * features // bands // HSZ, sources * bands, HSZ), jnp.float32),
        ],
        cost_estimate=pl.CostEstimate(
            flops=2 * token_rows * features * model, bytes_accessed=6 << 20, transcendentals=0
        ),
        name="pack",
    )(device.reshape(1), bucket_grid, queries, keys, values, grad_out, w_out)
    arrived = lax.all_to_all(packed, SEQ, split_axis=0, concat_axis=0, tiled=True)
    arrived = arrived.reshape(slot_rows, 4 * features)

    width = model // heads
    w_blocks = [
        lax.dynamic_slice_in_dim(w_out, (head + k) % heads * width, width, axis=1)
        for k in range(heads)
    ]
    w_mine = [
        shifted(w_blocks[k], "head", k) if k in (1, heads - 1) else w_blocks[k]
        for k in range(heads)
    ]

    where_here, alive_here = member_table(bucket_grid, device, slot_total)
    where_before, alive_before = member_table(bucket_grid, device - 1, slot_total)
    query_at = jnp.where(alive_here > 0, where_here, -1)[:, None]
    key_at = jnp.concatenate(
        [
            jnp.where(alive_here > 0, where_here, NEVER),
            jnp.where(alive_before > 0, where_before, NEVER),
        ]
    )[None, :]

    chunks = grad_out.reshape(token_rows, depth, cols, model // (depth * cols))
    out_blocks = jnp.moveaxis(chunks, 2, 0).reshape(cols, token_rows, model // cols)
    outs = [lax.dynamic_index_in_dim(out_blocks, col, 0, keepdims=False)]
    for k in range(1, cols):
        block = lax.dynamic_index_in_dim(out_blocks, (col + k) % cols, 0, keepdims=False)
        outs.append(shifted(block, "seq_1", k))
    arrived, query_at, key_at, back, mine, *outs = lax.optimization_barrier(
        (arrived, query_at, key_at, back, mine, *outs)
    )

    prev = passed_along(arrived[:, features : 3 * features], SEQ, 1)
    prev, w_mine[1], w_mine[-1] = lax.optimization_barrier((prev, w_mine[1], w_mine[-1]))
    products = 2 * groups * slot_rows * 2 * slot_rows * HSZ
    lanes = -(-slot_total * groups // bands) * HSZ
    pair = (slot_rows, 2 * features)
    attended, grad_query, own_terms, prev_terms = pl.pallas_call(
        functools.partial(bucket_kernel, scaling, slot_total),
        out_shape=(
            jax.ShapeDtypeStruct((sources, bands, lanes), jnp.bfloat16),
            jax.ShapeDtypeStruct((slot_rows, features), jnp.bfloat16),
            jax.ShapeDtypeStruct(pair, jnp.float32),
            jax.ShapeDtypeStruct(pair, jnp.bfloat16),
        ),
        scratch_shapes=[
            pltpu.VMEM((slot_rows, HSZ), jnp.float32),
            pltpu.VMEM((lanes // HSZ, sources * bands, HSZ), jnp.float32),
        ],
        cost_estimate=pl.CostEstimate(
            flops=6 * products, bytes_accessed=3 << 20, transcendentals=0
        ),
        name="bucket",
    )(arrived, prev, query_at, key_at)
    attended, w_mine[2], *outs = lax.optimization_barrier((attended, w_blocks[2], *outs))
    pair_next = passed_along(prev_terms, SEQ, -1)
    w_mine[2] = shifted(w_mine[2], "head", 2)
    outs = outs + [shifted(block, "seq_2", 1) for block in outs]
    returned = lax.all_to_all(attended, SEQ, split_axis=0, concat_axis=0, tiled=True)
    pair_total = (own_terms + pair_next.astype(jnp.float32)).astype(jnp.bfloat16)
    grads = jnp.concatenate([grad_query, pair_total], axis=1)
    grads = grads.reshape(sources, 4, slot_total * 3 * features // 4)
    returned, grads, *outs = lax.optimization_barrier((returned, grads, *outs))
    returned_grads = lax.all_to_all(grads, SEQ, split_axis=0, concat_axis=0, tiled=True)
    half = features // 2
    halves = jax.ShapeDtypeStruct((token_rows, half), jnp.bfloat16)
    home, keep, give = pl.pallas_call(
        functools.partial(home_kernel, slot_total),
        in_specs=[pl.BlockSpec(memory_space=pltpu.SMEM)]
        + [pl.BlockSpec(memory_space=pltpu.VMEM)] * 2,
        out_shape=(jax.ShapeDtypeStruct((token_rows, features), jnp.bfloat16), halves, halves),
        scratch_shapes=[pltpu.VMEM((lanes // HSZ, sources * bands, HSZ), jnp.float32)],
        cost_estimate=pl.CostEstimate(flops=1 << 26, bytes_accessed=2 << 20, transcendentals=0),
        name="home",
    )(core.reshape(1), mine[None, :], returned)
    both = jnp.stack([keep, shifted(give, "seq_2", 1)])
    rows = [both] + [shifted(both, "seq_1", k) for k in range(1, cols)]

    homes = [home] + [shifted(home, "head", k) for k in range(1, heads)]

    share = model // cols // depth
    kept, *sent = pl.pallas_call(
        functools.partial(weight_kernel, cols, depth),
        in_specs=[pl.BlockSpec(memory_space=pltpu.SMEM)]
        + [pl.BlockSpec(memory_space=pltpu.VMEM)] * (3 * cols),
        out_shape=[jax.ShapeDtypeStruct((half, share), jnp.float32)]
        + [jax.ShapeDtypeStruct((half, share), jnp.bfloat16)] * (depth - 1),
        scratch_shapes=[pltpu.VMEM((half, model // cols), jnp.float32)],
        cost_estimate=pl.CostEstimate(
            flops=2 * half * model * 2 * token_rows, bytes_accessed=4 << 20, transcendentals=0
        ),
        name="weight",
    )(lax.axis_index("seq_0").reshape(1), *outs, *rows)
    sent = [shifted(sent[k - 1], "seq_0", k) for k in range(1, depth)]
    summed = kept
    for block in sent:
        summed = summed + block.astype(jnp.float32)
    layer_out = sum(product(homes[k], w_mine[k]) for k in range(heads)).astype(jnp.bfloat16)
    low, high = summed[:, : share // 2], summed[:, share // 2 :]
    keep = jnp.where(core == 0, low, high)
    got = shifted(jnp.where(core == 0, high, low), "seq_2", 1)
    grad_weight = jnp.concatenate(
        [jnp.where(core == 0, keep, got), jnp.where(core == 0, got, keep)], axis=0
    )

    back_all = picked(back, returned_grads.reshape(slot_rows, 3 * features))
    grad_queries = back_all[:, :features]
    grad_keys = back_all[:, features : 2 * features]
    grad_values = back_all[:, 2 * features :]
    return (layer_out, grad_queries, grad_keys, grad_values, grad_weight)


def solution(mesh):
    finer = Mesh(
        mesh.devices.reshape(8, 4, 2, mesh.shape["head"]), ("seq_0", "seq_1", "seq_2", "head")
    )
    placed = (P(SEQ, "head"), P(SEQ, "head"), P(SEQ, "head"), P(), P("head", None), P(SEQ, None))
    return jax.shard_map(
        per_device,
        mesh=finer,
        in_specs=placed,
        out_specs=(P(SEQ, "head"), P(SEQ, "head"), P(SEQ, "head"), P(SEQ, "head"), P("head", SEQ)),
        check_vma=False,
    )
```

```python
import functools
import math

import jax
import jax.numpy as jnp
from jax import lax
from jax.experimental import pallas as pl
from jax.experimental.pallas import tpu as pltpu
from jax.sharding import Mesh
from jax.sharding import PartitionSpec as P


HSZ = 128
SEQ = ("seq_0", "seq_1", "seq_2")


def shifted(value, axis, by):
    length = lax.axis_size(axis)
    return lax.ppermute(value, axis, [(i, (i + by) % length) for i in range(length)])


def passed_along(value, axis, by):
    length = lax.axis_size(axis)
    pairs = [(i, i + by) for i in range(length) if 0 <= i + by < length]
    return lax.ppermute(value, axis, pairs)


def member_table(bucket_grid, owner, slot_count):
    sources, stride = bucket_grid.shape
    matches = bucket_grid == owner
    token = jnp.arange(stride)
    earlier = (token[:, None] < token[None, :]).astype(jnp.bfloat16)
    ranking = jnp.dot(matches.astype(jnp.bfloat16), earlier, preferred_element_type=jnp.float32)
    offsets = (
        jnp.arange(sources, dtype=jnp.int32)[:, None] * stride
        + jnp.arange(stride, dtype=jnp.int32)[None, :]
    )
    where_at = []
    present = []
    for slot in range(slot_count):
        placed = (matches & (ranking == slot)).astype(jnp.int32)
        where_at.append(jnp.sum(placed * offsets, axis=1))
        present.append(jnp.sum(placed, axis=1))
    return (jnp.stack(where_at, axis=1).reshape(-1), jnp.stack(present, axis=1).reshape(-1))


NEVER = 1 << 30
NT = (((1,), (1,)), ((), ()))
TN = (((0,), (0,)), ((), ()))


def product(left, right, dims=(((1,), (0,)), ((), ()))):
    return lax.dot_general(left, right, dims, preferred_element_type=jnp.float32)


def hidden(query_at, key_at):
    slots = query_at.shape[0]
    seen = key_at <= query_at
    row = lax.broadcasted_iota(jnp.int32, (slots, 2 * slots), 0)
    column = lax.broadcasted_iota(jnp.int32, (slots, 2 * slots), 1)
    return jnp.where(seen | (row == column), 0.0, -1e30)


def probs_of(query, key_here, key_before, bias, scaling):
    slots = query.shape[0]
    here = product(query, key_here, NT) * scaling + bias[:, :slots]
    before = product(query, key_before, NT) * scaling + bias[:, slots:]
    largest = jnp.maximum(
        jnp.max(here, axis=1, keepdims=True), jnp.max(before, axis=1, keepdims=True)
    )
    here = jnp.exp(here - largest)
    before = jnp.exp(before - largest)
    total = jnp.sum(here, axis=1, keepdims=True) + jnp.sum(before, axis=1, keepdims=True)
    inverse = 1.0 / total
    return here * inverse, before * inverse


def bucket_kernel(
    scaling,
    slot_total,
    rows,
    prev,
    query_at,
    key_at,
    attended,
    grad_query,
    own_terms,
    prev_terms,
    held,
    spread,
):
    features = rows.shape[1] // 4
    heads = features // HSZ
    count, bands = attended.shape[0], attended.shape[1]
    tiles = spread.shape[0]
    bias = hidden(query_at[...], key_at[...])
    spread[...] = jnp.zeros(spread.shape, jnp.float32)
    for head in range(heads):
        def part(ref, index):
            return ref[:, index * features + head * HSZ : index * features + (head + 1) * HSZ]

        query, key, value, grad = (part(rows, index) for index in range(4))
        key_prev, value_prev = part(prev, 0), part(prev, 1)
        here, before = probs_of(query, key, key_prev, bias, scaling)
        here_b = here.astype(jnp.bfloat16)
        before_b = before.astype(jnp.bfloat16)
        out = product(here_b, value) + product(before_b, value_prev)
        held[...] = out
        for slot in range(slot_total):
            chunk = slot * heads + head
            spread[chunk % tiles, pl.ds(chunk // tiles, count, stride=bands), :] = held[
                pl.ds(slot, count, stride=slot_total), :
            ]
        out = out.astype(jnp.bfloat16).astype(jnp.float32)
        centre = jnp.sum(out * grad.astype(jnp.float32), axis=1, keepdims=True)
        d_here = (here * (product(grad, value, NT) - centre)).astype(jnp.bfloat16)
        d_before = (before * (product(grad, value_prev, NT) - centre)).astype(jnp.bfloat16)
        start, end = head * HSZ, (head + 1) * HSZ
        to_query = (product(d_here, key) + product(d_before, key_prev)) * scaling
        grad_query[:, start:end] = to_query.astype(jnp.bfloat16)
        own_terms[:, start:end] = product(d_here, query, TN) * scaling
        own_terms[:, features + start : features + end] = product(here_b, grad, TN)
        prev_terms[:, start:end] = (product(d_before, query, TN) * scaling).astype(jnp.bfloat16)
        prev_terms[:, features + start : features + end] = product(before_b, grad, TN).astype(
            jnp.bfloat16
        )
    for tile in range(tiles):
        attended[:, :, tile * HSZ : (tile + 1) * HSZ] = (
            spread[tile].reshape(count, bands, HSZ).astype(jnp.bfloat16)
        )


def weight_kernel(cols, depth, place, *refs):
    outs = refs[: 2 * cols]
    rows = refs[2 * cols : 3 * cols]
    kept = refs[3 * cols]
    sent = refs[3 * cols + 1 : 3 * cols + depth]
    total = refs[-1]
    columns = total.shape[1]
    step = 256
    for start in range(0, columns, step):
        acc = None
        for k in range(cols):
            for side in range(2):
                term = product(rows[k][side], outs[side * cols + k][:, start : start + step], TN)
                acc = term if acc is None else acc + term
        total[:, start : start + step] = acc
    width = columns // depth
    for k in range(depth):
        at = lax.rem(place[0] + k, depth)
        block = total[:, pl.ds(pl.multiple_of(at * width, width), width)]
        if k == 0:
            kept[...] = block
        else:
            sent[k - 1][...] = block.astype(jnp.bfloat16)


def home_kernel(slot_total, core, picks, returned, home, keep, give, spread):
    count, bands, lanes = returned.shape
    _, features = home.shape
    heads = features // HSZ
    tiles = lanes // HSZ
    used = min(tiles, slot_total * heads)
    for tile in range(used):
        block = returned[:, :, tile * HSZ : (tile + 1) * HSZ]
        spread[tile] = block.astype(jnp.float32).reshape(count * bands, HSZ)
    for head in range(heads):
        total = None
        for slot in range(slot_total):
            chunk = slot * heads + head
            rows = spread[chunk % tiles, pl.ds(chunk // tiles, count, stride=bands), :]
            term = product(picks[slot], rows.astype(jnp.bfloat16))
            total = term if total is None else total + term
        home[:, head * HSZ : (head + 1) * HSZ] = total.astype(jnp.bfloat16)
    half = features // 2
    keep[...] = home[:, pl.ds(pl.multiple_of(core[0] * half, HSZ), half)]
    give[...] = home[:, pl.ds(pl.multiple_of((1 - core[0]) * half, HSZ), half)]


def layer_kernel(count, _, *refs):
    homes, weights, out = refs[:count], refs[count : 2 * count], refs[-1]
    total = product(homes[0][...], weights[0][...])
    for k in range(1, count):
        total = total + product(homes[k][...], weights[k][...])
    out[...] = total.astype(jnp.bfloat16)


def pack_kernel(slot_total, device, grid, queries, keys, values, out, weight, packed, total, spread, chosen):
    step = pl.program_id(0)
    term = product(out[...], weight[...], NT)

    @pl.when(step == 0)
    def _():
        total[...] = term

    @pl.when(step > 0)
    def _():
        total[...] += term

    tokens, features = queries.shape
    count, bands = packed.shape[0], packed.shape[1]
    tiles = spread.shape[0]

    def place(index, source):
        rows = product(chosen[...], source)
        for part in range(features // HSZ):
            for slot in range(slot_total):
                chunk = (slot * 4 + index) * (features // HSZ) + part
                spread[chunk % tiles, pl.ds(chunk // tiles, count, stride=bands), :] = rows[
                    slot * count : (slot + 1) * count, part * HSZ : (part + 1) * HSZ
                ]

    @pl.when(step == 0)
    def _():
        row = lax.broadcasted_iota(jnp.int32, (tokens, tokens), 0)
        column = lax.broadcasted_iota(jnp.int32, (tokens, tokens), 1)
        mine = grid[pl.ds(device[0], 1), :]
        named = jnp.broadcast_to(mine, (tokens, tokens))
        same = (named == named.T) & (row < column)
        ranking = jnp.sum(same.astype(jnp.int32), axis=0, keepdims=True)
        slot_of = ranking * count + mine
        slots = lax.broadcasted_iota(jnp.int32, (slot_total * count, tokens), 0)
        chosen[...] = jnp.where(slots == slot_of, 1.0, 0.0).astype(jnp.bfloat16)

    for index, source in enumerate((queries, keys, values)):

        @pl.when(step == index)
        def _(index=index, source=source):
            place(index, source[...])

    @pl.when(step == pl.num_programs(0) - 1)
    def _():
        place(3, total[...].astype(jnp.bfloat16))
        for tile in range(tiles):
            packed[:, :, tile * HSZ : (tile + 1) * HSZ] = (
                spread[tile].reshape(count, bands, HSZ).astype(jnp.bfloat16)
            )


def slot_matrix(mine, slot_total, count):
    token = jnp.arange(mine.shape[0])
    same = (mine[:, None] == mine[None, :]) & (token[None, :] < token[:, None])
    ranking = jnp.sum(same.astype(jnp.int32), axis=1)
    owner = jnp.arange(count)[None, :]
    picks = jnp.stack(
        [
            ((mine[:, None] == owner) & (ranking[:, None] == k)).astype(jnp.bfloat16)
            for k in range(slot_total)
        ]
    )
    slot = jnp.arange(count * slot_total)[None, :]
    back = (slot == (mine * slot_total + ranking)[:, None]).astype(jnp.bfloat16)
    return back, picks


def picked(selection, rows):
    return jnp.dot(selection, rows, preferred_element_type=jnp.float32).astype(jnp.bfloat16)


def per_device(queries, keys, values, bucket, w_out, grad_out):
    sources = lax.axis_size(SEQ)
    device = lax.axis_index(SEQ)
    col = lax.axis_index("seq_1")
    core = lax.axis_index("seq_2")
    head = lax.axis_index("head")
    cols = lax.axis_size("seq_1")
    depth = lax.axis_size("seq_0")
    heads = lax.axis_size("head")
    token_rows, features = queries.shape
    model = grad_out.shape[1]
    groups = features // HSZ
    slot_total = max(2, 3 * token_rows // (2 * sources))
    slot_rows = sources * slot_total
    scaling = 1.0 / math.sqrt(HSZ)
    bucket_grid = bucket[:, 0].reshape(sources, token_rows)
    mine = lax.dynamic_index_in_dim(bucket_grid, device, 0, keepdims=False)
    back, picks = slot_matrix(mine, slot_total, sources)
    bands = 8
    split = 4
    whole = pl.BlockSpec((token_rows, features), lambda k: (0, 0))
    packed = pl.pallas_call(
        functools.partial(pack_kernel, slot_total),
        grid=(split,),
        in_specs=[
            pl.BlockSpec(memory_space=pltpu.SMEM),
            pl.BlockSpec((sources, token_rows), lambda k: (0, 0)),
            whole,
            whole,
            whole,
            pl.BlockSpec((token_rows, model // split), lambda k: (0, k)),
            pl.BlockSpec((features, model // split), lambda k: (0, k)),
        ],
        out_specs=pl.BlockSpec(
            (sources, bands, slot_total * 4 * features // bands), lambda k: (0, 0, 0)
        ),
        out_shape=jax.ShapeDtypeStruct(
            (sources, bands, slot_total * 4 * features // bands), jnp.bfloat16
        ),
        scratch_shapes=[
            pltpu.VMEM((token_rows, features), jnp.float32),
            pltpu.VMEM((slot_total * 4 * features // bands // HSZ, sources * bands, HSZ), jnp.float32),
            pltpu.VMEM((slot_rows, token_rows), jnp.bfloat16),
        ],
        cost_estimate=pl.CostEstimate(
            flops=2 * token_rows * features * model, bytes_accessed=6 << 20, transcendentals=0
        ),
        name="pack",
    )(device.reshape(1), bucket_grid, queries, keys, values, grad_out, w_out)
    arrived = lax.all_to_all(packed, SEQ, split_axis=0, concat_axis=0, tiled=True)
    arrived = arrived.reshape(slot_rows, 4 * features)

    width = model // heads
    w_blocks = [
        lax.dynamic_slice_in_dim(w_out, (head + k) % heads * width, width, axis=1)
        for k in range(heads)
    ]
    w_mine = [
        shifted(w_blocks[k], "head", k) if k in (1, heads - 1) else w_blocks[k]
        for k in range(heads)
    ]

    where_here, alive_here = member_table(bucket_grid, device, slot_total)
    where_before, alive_before = member_table(bucket_grid, device - 1, slot_total)
    query_at = jnp.where(alive_here > 0, where_here, -1)[:, None]
    key_at = jnp.concatenate(
        [
            jnp.where(alive_here > 0, where_here, NEVER),
            jnp.where(alive_before > 0, where_before, NEVER),
        ]
    )[None, :]

    chunks = grad_out.reshape(token_rows, depth, cols, model // (depth * cols))
    out_blocks = jnp.moveaxis(chunks, 2, 0).reshape(cols, token_rows, model // cols)
    outs = [lax.dynamic_index_in_dim(out_blocks, col, 0, keepdims=False)]
    for k in range(1, cols):
        block = lax.dynamic_index_in_dim(out_blocks, (col + k) % cols, 0, keepdims=False)
        outs.append(shifted(block, "seq_1", k))
    arrived, query_at, key_at, back, picks, *outs = lax.optimization_barrier(
        (arrived, query_at, key_at, back, picks, *outs)
    )

    prev = passed_along(arrived[:, features : 3 * features], SEQ, 1)
    products = 2 * groups * slot_rows * 2 * slot_rows * HSZ
    lanes = -(-slot_total * groups // bands) * HSZ
    pair = (slot_rows, 2 * features)
    attended, grad_query, own_terms, prev_terms = pl.pallas_call(
        functools.partial(bucket_kernel, scaling, slot_total),
        out_shape=(
            jax.ShapeDtypeStruct((sources, bands, lanes), jnp.bfloat16),
            jax.ShapeDtypeStruct((slot_rows, features), jnp.bfloat16),
            jax.ShapeDtypeStruct(pair, jnp.float32),
            jax.ShapeDtypeStruct(pair, jnp.bfloat16),
        ),
        scratch_shapes=[
            pltpu.VMEM((slot_rows, HSZ), jnp.float32),
            pltpu.VMEM((lanes // HSZ, sources * bands, HSZ), jnp.float32),
        ],
        cost_estimate=pl.CostEstimate(
            flops=6 * products, bytes_accessed=3 << 20, transcendentals=0
        ),
        name="bucket",
    )(arrived, prev, query_at, key_at)
    attended, *moved = lax.optimization_barrier((attended, *w_mine, *outs))
    w_mine, outs = moved[:heads], moved[heads:]
    pair_next = passed_along(prev_terms, SEQ, -1)
    w_mine[2] = shifted(w_mine[2], "head", 2)
    outs = outs + [shifted(block, "seq_2", 1) for block in outs]
    returned = lax.all_to_all(attended, SEQ, split_axis=0, concat_axis=0, tiled=True)
    pair_total = (own_terms + pair_next.astype(jnp.float32)).astype(jnp.bfloat16)
    grads = jnp.concatenate([grad_query, pair_total], axis=1)
    grads = grads.reshape(sources, 4, slot_total * 3 * features // 4)
    returned, grads, *outs = lax.optimization_barrier((returned, grads, *outs))
    returned_grads = lax.all_to_all(grads, SEQ, split_axis=0, concat_axis=0, tiled=True)
    half = features // 2
    halves = jax.ShapeDtypeStruct((token_rows, half), jnp.bfloat16)
    pick_home = pl.pallas_call(
        functools.partial(home_kernel, slot_total),
        in_specs=[pl.BlockSpec(memory_space=pltpu.SMEM)]
        + [pl.BlockSpec(memory_space=pltpu.VMEM)] * 2,
        out_shape=(jax.ShapeDtypeStruct((token_rows, features), jnp.bfloat16), halves, halves),
        scratch_shapes=[pltpu.VMEM((lanes // HSZ, sources * bands, HSZ), jnp.float32)],
        cost_estimate=pl.CostEstimate(flops=1 << 26, bytes_accessed=2 << 20, transcendentals=0),
        name="home",
    )
    home, keep, give = pick_home(core.reshape(1), picks, returned)
    both = jnp.stack([keep, shifted(give, "seq_2", 1)])
    rows = [both] + [shifted(both, "seq_1", k) for k in range(1, cols)]

    homes = [home] + [shifted(home, "head", k) for k in range(1, heads)]

    share = model // cols // depth
    kept, *sent = pl.pallas_call(
        functools.partial(weight_kernel, cols, depth),
        in_specs=[pl.BlockSpec(memory_space=pltpu.SMEM)]
        + [pl.BlockSpec(memory_space=pltpu.VMEM)] * (3 * cols),
        out_shape=[jax.ShapeDtypeStruct((half, share), jnp.float32)]
        + [jax.ShapeDtypeStruct((half, share), jnp.bfloat16)] * (depth - 1),
        scratch_shapes=[pltpu.VMEM((half, model // cols), jnp.float32)],
        cost_estimate=pl.CostEstimate(
            flops=2 * half * model * 2 * token_rows, bytes_accessed=4 << 20, transcendentals=0
        ),
        name="weight",
    )(lax.axis_index("seq_0").reshape(1), *outs, *rows)
    far = sorted(range(1, depth), key=lambda k: abs(2 * k - depth))
    sent = [shifted(sent[k - 1], "seq_0", k) for k in far]
    summed = kept
    for block in sent:
        summed = summed + block.astype(jnp.float32)
    strip = 256
    parts = width // strip
    layer_out = pl.pallas_call(
        functools.partial(layer_kernel, heads),
        grid_spec=pltpu.PrefetchScalarGridSpec(
            num_scalar_prefetch=1,
            grid=(parts,),
            in_specs=[pl.BlockSpec((token_rows, features), lambda i, at: (0, 0))] * heads
            + [pl.BlockSpec((features, strip), lambda i, at: (0, at[0] * parts + i))]
            + [pl.BlockSpec((features, strip), lambda i, at: (0, i))] * (heads - 1),
            out_specs=pl.BlockSpec((token_rows, strip), lambda i, at: (0, i)),
        ),
        out_shape=jax.ShapeDtypeStruct((token_rows, width), jnp.bfloat16),
        cost_estimate=pl.CostEstimate(
            flops=2 * token_rows * features * model, bytes_accessed=5 << 20, transcendentals=0
        ),
        name="layer",
    )(head.reshape(1), *homes, w_out, *w_mine[1:])
    low, high = summed[:, : share // 2], summed[:, share // 2 :]
    keep = jnp.where(core == 0, low, high)
    got = shifted(jnp.where(core == 0, high, low), "seq_2", 1)
    grad_weight = jnp.concatenate(
        [jnp.where(core == 0, keep, got), jnp.where(core == 0, got, keep)], axis=0
    )

    back_all = picked(back, returned_grads.reshape(slot_rows, 3 * features))
    grad_queries = back_all[:, :features]
    grad_keys = back_all[:, features : 2 * features]
    grad_values = back_all[:, 2 * features :]
    return (layer_out, grad_queries, grad_keys, grad_values, grad_weight)


def solution(mesh):
    finer = Mesh(
        mesh.devices.reshape(8, 4, 2, mesh.shape["head"]), ("seq_0", "seq_1", "seq_2", "head")
    )
    placed = (P(SEQ, "head"), P(SEQ, "head"), P(SEQ, "head"), P(), P("head", None), P(SEQ, None))
    return jax.shard_map(
        per_device,
        mesh=finer,
        in_specs=placed,
        out_specs=(P(SEQ, "head"), P(SEQ, "head"), P(SEQ, "head"), P(SEQ, "head"), P("head", SEQ)),
        check_vma=False,
    )
```

```python
import functools
import math

import jax
import jax.numpy as jnp
from jax import lax
from jax.experimental import pallas as pl
from jax.experimental.pallas import tpu as pltpu
from jax.sharding import Mesh
from jax.sharding import PartitionSpec as P


HSZ = 128
SEQ = ("seq_0", "seq_1", "seq_2")


def shifted(value, axis, by):
    length = lax.axis_size(axis)
    return lax.ppermute(value, axis, [(i, (i + by) % length) for i in range(length)])


def passed_along(value, axis, by):
    length = lax.axis_size(axis)
    pairs = [(i, i + by) for i in range(length) if 0 <= i + by < length]
    return lax.ppermute(value, axis, pairs)


def member_table(bucket_grid, owner, slot_count):
    sources, stride = bucket_grid.shape
    matches = bucket_grid == owner
    token = jnp.arange(stride)
    earlier = (token[:, None] < token[None, :]).astype(jnp.bfloat16)
    ranking = jnp.dot(matches.astype(jnp.bfloat16), earlier, preferred_element_type=jnp.float32)
    offsets = (
        jnp.arange(sources, dtype=jnp.int32)[:, None] * stride
        + jnp.arange(stride, dtype=jnp.int32)[None, :]
    )
    where_at = []
    present = []
    for slot in range(slot_count):
        placed = (matches & (ranking == slot)).astype(jnp.int32)
        where_at.append(jnp.sum(placed * offsets, axis=1))
        present.append(jnp.sum(placed, axis=1))
    return (jnp.stack(where_at, axis=1).reshape(-1), jnp.stack(present, axis=1).reshape(-1))


NEVER = 1 << 30
NT = (((1,), (1,)), ((), ()))
TN = (((0,), (0,)), ((), ()))


def product(left, right, dims=(((1,), (0,)), ((), ()))):
    return lax.dot_general(left, right, dims, preferred_element_type=jnp.float32)


def hidden(query_at, key_at):
    slots = query_at.shape[0]
    seen = key_at <= query_at
    row = lax.broadcasted_iota(jnp.int32, (slots, 2 * slots), 0)
    column = lax.broadcasted_iota(jnp.int32, (slots, 2 * slots), 1)
    return jnp.where(seen | (row == column), 0.0, -1e30)


def probs_of(query, key_here, key_before, bias, scaling):
    slots = query.shape[0]
    here = product(query, key_here, NT) * scaling + bias[:, :slots]
    before = product(query, key_before, NT) * scaling + bias[:, slots:]
    largest = jnp.maximum(
        jnp.max(here, axis=1, keepdims=True), jnp.max(before, axis=1, keepdims=True)
    )
    here = jnp.exp(here - largest)
    before = jnp.exp(before - largest)
    total = jnp.sum(here, axis=1, keepdims=True) + jnp.sum(before, axis=1, keepdims=True)
    inverse = 1.0 / total
    return here * inverse, before * inverse


def bucket_kernel(
    scaling,
    slot_total,
    rows,
    pairs,
    prev,
    query_at,
    key_at,
    attended,
    grad_query,
    own_terms,
    prev_terms,
    held,
    spread,
):
    features = rows.shape[1] // 2
    heads = features // HSZ
    count, bands = attended.shape[0], attended.shape[1]
    tiles = spread.shape[0]
    bias = hidden(query_at[...], key_at[...])
    spread[...] = jnp.zeros(spread.shape, jnp.float32)
    for head in range(heads):
        def part(ref, index):
            return ref[:, index * features + head * HSZ : index * features + (head + 1) * HSZ]

        query, grad = part(rows, 0), part(rows, 1)
        key, value = part(pairs, 0), part(pairs, 1)
        key_prev, value_prev = part(prev, 0), part(prev, 1)
        here, before = probs_of(query, key, key_prev, bias, scaling)
        here_b = here.astype(jnp.bfloat16)
        before_b = before.astype(jnp.bfloat16)
        out = product(here_b, value) + product(before_b, value_prev)
        held[...] = out
        for slot in range(slot_total):
            chunk = slot * heads + head
            spread[chunk % tiles, pl.ds(chunk // tiles, count, stride=bands), :] = held[
                pl.ds(slot, count, stride=slot_total), :
            ]
        out = out.astype(jnp.bfloat16).astype(jnp.float32)
        centre = jnp.sum(out * grad.astype(jnp.float32), axis=1, keepdims=True)
        d_here = (here * (product(grad, value, NT) - centre)).astype(jnp.bfloat16)
        d_before = (before * (product(grad, value_prev, NT) - centre)).astype(jnp.bfloat16)
        start, end = head * HSZ, (head + 1) * HSZ
        to_query = (product(d_here, key) + product(d_before, key_prev)) * scaling
        grad_query[:, start:end] = to_query.astype(jnp.bfloat16)
        own_terms[:, start:end] = product(d_here, query, TN) * scaling
        own_terms[:, features + start : features + end] = product(here_b, grad, TN)
        prev_terms[:, start:end] = (product(d_before, query, TN) * scaling).astype(jnp.bfloat16)
        prev_terms[:, features + start : features + end] = product(before_b, grad, TN).astype(
            jnp.bfloat16
        )
    for tile in range(tiles):
        attended[:, :, tile * HSZ : (tile + 1) * HSZ] = (
            spread[tile].reshape(count, bands, HSZ).astype(jnp.bfloat16)
        )


def weight_kernel(cols, depth, place, *refs):
    outs = refs[: 2 * cols]
    rows = refs[2 * cols : 3 * cols]
    kept = refs[3 * cols]
    sent = refs[3 * cols + 1 : 3 * cols + depth]
    total = refs[-1]
    columns = total.shape[1]
    step = 256
    for start in range(0, columns, step):
        acc = None
        for k in range(cols):
            for side in range(2):
                term = product(rows[k][side], outs[side * cols + k][:, start : start + step], TN)
                acc = term if acc is None else acc + term
        total[:, start : start + step] = acc
    width = columns // depth
    for k in range(depth):
        at = lax.rem(place[0] + k, depth)
        block = total[:, pl.ds(pl.multiple_of(at * width, width), width)]
        if k == 0:
            kept[...] = block
        else:
            sent[k - 1][...] = block.astype(jnp.bfloat16)


def home_kernel(slot_total, core, picks, returned, home, keep, give, spread):
    count, bands, lanes = returned.shape
    _, features = home.shape
    heads = features // HSZ
    tiles = lanes // HSZ
    used = min(tiles, slot_total * heads)
    for tile in range(used):
        block = returned[:, :, tile * HSZ : (tile + 1) * HSZ]
        spread[tile] = block.astype(jnp.float32).reshape(count * bands, HSZ)
    for head in range(heads):
        total = None
        for slot in range(slot_total):
            chunk = slot * heads + head
            rows = spread[chunk % tiles, pl.ds(chunk // tiles, count, stride=bands), :]
            term = product(picks[slot], rows.astype(jnp.bfloat16))
            total = term if total is None else total + term
        home[:, head * HSZ : (head + 1) * HSZ] = total.astype(jnp.bfloat16)
    half = features // 2
    keep[...] = home[:, pl.ds(pl.multiple_of(core[0] * half, HSZ), half)]
    give[...] = home[:, pl.ds(pl.multiple_of((1 - core[0]) * half, HSZ), half)]


def layer_kernel(count, *refs):
    homes, weights, out = refs[:count], refs[count : 2 * count], refs[-1]
    strip = 256
    for start in range(0, out.shape[1], strip):
        total = None
        for k in range(count):
            term = product(homes[k][...], weights[k][:, start : start + strip])
            total = term if total is None else total + term
        out[:, start : start + strip] = total.astype(jnp.bfloat16)


def pack_kernel(slot_total, device, grid, queries, keys, values, out, weight, packed, total, spread, chosen):
    step = pl.program_id(0)
    term = product(out[...], weight[...], NT)

    @pl.when(step == 0)
    def _():
        total[...] = term

    @pl.when(step > 0)
    def _():
        total[...] += term

    tokens, features = queries.shape
    count, bands = packed.shape[0], packed.shape[1]
    tiles = spread.shape[0]

    def place(index, source):
        rows = product(chosen[...], source)
        for part in range(features // HSZ):
            for slot in range(slot_total):
                chunk = (index // 2 * slot_total + slot) * 2 + index % 2
                chunk = chunk * (features // HSZ) + part
                spread[chunk % tiles, pl.ds(chunk // tiles, count, stride=bands), :] = rows[
                    slot * count : (slot + 1) * count, part * HSZ : (part + 1) * HSZ
                ]

    @pl.when(step == 0)
    def _():
        row = lax.broadcasted_iota(jnp.int32, (tokens, tokens), 0)
        column = lax.broadcasted_iota(jnp.int32, (tokens, tokens), 1)
        mine = grid[pl.ds(device[0], 1), :]
        named = jnp.broadcast_to(mine, (tokens, tokens))
        same = (named == named.T) & (row < column)
        ranking = jnp.sum(same.astype(jnp.int32), axis=0, keepdims=True)
        slot_of = ranking * count + mine
        slots = lax.broadcasted_iota(jnp.int32, (slot_total * count, tokens), 0)
        chosen[...] = jnp.where(slots == slot_of, 1.0, 0.0).astype(jnp.bfloat16)

    for index, source in enumerate((keys, values, queries)):

        @pl.when(step == index)
        def _(index=index, source=source):
            place(index, source[...])

    @pl.when(step == pl.num_programs(0) - 1)
    def _():
        place(3, total[...].astype(jnp.bfloat16))
        for tile in range(tiles):
            packed[:, :, tile * HSZ : (tile + 1) * HSZ] = (
                spread[tile].reshape(count, bands, HSZ).astype(jnp.bfloat16)
            )


def slot_matrix(mine, slot_total, count):
    token = jnp.arange(mine.shape[0])
    same = (mine[:, None] == mine[None, :]) & (token[None, :] < token[:, None])
    ranking = jnp.sum(same.astype(jnp.int32), axis=1)
    owner = jnp.arange(count)[None, :]
    picks = jnp.stack(
        [
            ((mine[:, None] == owner) & (ranking[:, None] == k)).astype(jnp.bfloat16)
            for k in range(slot_total)
        ]
    )
    slot = jnp.arange(count * slot_total)[None, :]
    back = (slot == (mine * slot_total + ranking)[:, None]).astype(jnp.bfloat16)
    return back, picks


def picked(selection, rows):
    return jnp.dot(selection, rows, preferred_element_type=jnp.float32).astype(jnp.bfloat16)


def per_device(queries, keys, values, bucket, w_out, grad_out):
    sources = lax.axis_size(SEQ)
    device = lax.axis_index(SEQ)
    col = lax.axis_index("seq_1")
    core = lax.axis_index("seq_2")
    head = lax.axis_index("head")
    cols = lax.axis_size("seq_1")
    depth = lax.axis_size("seq_0")
    heads = lax.axis_size("head")
    token_rows, features = queries.shape
    model = grad_out.shape[1]
    groups = features // HSZ
    slot_total = max(2, 3 * token_rows // (2 * sources))
    slot_rows = sources * slot_total
    scaling = 1.0 / math.sqrt(HSZ)
    bucket_grid = bucket[:, 0].reshape(sources, token_rows)
    mine = lax.dynamic_index_in_dim(bucket_grid, device, 0, keepdims=False)
    back, picks = slot_matrix(mine, slot_total, sources)
    bands = 8
    split = 4
    whole = pl.BlockSpec((token_rows, features), lambda k: (0, 0))
    packed = pl.pallas_call(
        functools.partial(pack_kernel, slot_total),
        grid=(split,),
        in_specs=[
            pl.BlockSpec(memory_space=pltpu.SMEM),
            pl.BlockSpec((sources, token_rows), lambda k: (0, 0)),
            whole,
            whole,
            whole,
            pl.BlockSpec((token_rows, model // split), lambda k: (0, k)),
            pl.BlockSpec((features, model // split), lambda k: (0, k)),
        ],
        out_specs=pl.BlockSpec(
            (sources, bands, slot_total * 4 * features // bands), lambda k: (0, 0, 0)
        ),
        out_shape=jax.ShapeDtypeStruct(
            (sources, bands, slot_total * 4 * features // bands), jnp.bfloat16
        ),
        scratch_shapes=[
            pltpu.VMEM((token_rows, features), jnp.float32),
            pltpu.VMEM((slot_total * 4 * features // bands // HSZ, sources * bands, HSZ), jnp.float32),
            pltpu.VMEM((slot_rows, token_rows), jnp.bfloat16),
        ],
        cost_estimate=pl.CostEstimate(
            flops=2 * token_rows * features * model, bytes_accessed=6 << 20, transcendentals=0
        ),
        name="pack",
    )(device.reshape(1), bucket_grid, queries, keys, values, grad_out, w_out)
    arrived = lax.all_to_all(packed, SEQ, split_axis=0, concat_axis=0, tiled=True)

    width = model // heads
    w_blocks = [
        lax.dynamic_slice_in_dim(w_out, (head + k) % heads * width, width, axis=1)
        for k in range(heads)
    ]
    w_mine = [
        shifted(w_blocks[k], "head", k) if k in (1, heads - 1) else w_blocks[k]
        for k in range(heads)
    ]

    where_here, alive_here = member_table(bucket_grid, device, slot_total)
    where_before, alive_before = member_table(bucket_grid, device - 1, slot_total)
    query_at = jnp.where(alive_here > 0, where_here, -1)[:, None]
    key_at = jnp.concatenate(
        [
            jnp.where(alive_here > 0, where_here, NEVER),
            jnp.where(alive_before > 0, where_before, NEVER),
        ]
    )[None, :]

    chunks = grad_out.reshape(token_rows, depth, cols, model // (depth * cols))
    out_blocks = jnp.moveaxis(chunks, 2, 0).reshape(cols, token_rows, model // cols)
    outs = [lax.dynamic_index_in_dim(out_blocks, col, 0, keepdims=False)]
    for k in range(1, cols):
        block = lax.dynamic_index_in_dim(out_blocks, (col + k) % cols, 0, keepdims=False)
        outs.append(shifted(block, "seq_1", k))
    arrived, query_at, key_at, back, picks = lax.optimization_barrier(
        (arrived, query_at, key_at, back, picks)
    )
    pair_rows = arrived[:, : bands // 2].reshape(slot_rows, 2 * features)
    query_rows = arrived[:, bands // 2 :].reshape(slot_rows, 2 * features)

    prev = passed_along(pair_rows, SEQ, 1)
    products = 2 * groups * slot_rows * 2 * slot_rows * HSZ
    lanes = -(-slot_total * groups // bands) * HSZ
    pair = (slot_rows, 2 * features)
    attended, grad_query, own_terms, prev_terms = pl.pallas_call(
        functools.partial(bucket_kernel, scaling, slot_total),
        out_shape=(
            jax.ShapeDtypeStruct((sources, bands, lanes), jnp.bfloat16),
            jax.ShapeDtypeStruct((slot_rows, features), jnp.bfloat16),
            jax.ShapeDtypeStruct(pair, jnp.float32),
            jax.ShapeDtypeStruct(pair, jnp.bfloat16),
        ),
        scratch_shapes=[
            pltpu.VMEM((slot_rows, HSZ), jnp.float32),
            pltpu.VMEM((lanes // HSZ, sources * bands, HSZ), jnp.float32),
        ],
        cost_estimate=pl.CostEstimate(
            flops=6 * products, bytes_accessed=3 << 20, transcendentals=0
        ),
        name="bucket",
    )(query_rows, pair_rows, prev, query_at, key_at)
    attended, *moved = lax.optimization_barrier((attended, *w_mine, *outs))
    w_mine, outs = moved[:heads], moved[heads:]
    pair_next = passed_along(prev_terms, SEQ, -1)
    w_mine[2] = shifted(w_mine[2], "head", 2)
    outs = outs + [shifted(block, "seq_2", 1) for block in outs]
    returned = lax.all_to_all(attended, SEQ, split_axis=0, concat_axis=0, tiled=True)
    pair_total = (own_terms + pair_next.astype(jnp.float32)).astype(jnp.bfloat16)
    grads = jnp.concatenate([grad_query, pair_total], axis=1)
    grads = grads.reshape(sources, 4, slot_total * 3 * features // 4)
    returned, grads, *outs = lax.optimization_barrier((returned, grads, *outs))
    returned_grads = lax.all_to_all(grads, SEQ, split_axis=0, concat_axis=0, tiled=True)
    half = features // 2
    halves = jax.ShapeDtypeStruct((token_rows, half), jnp.bfloat16)
    pick_home = pl.pallas_call(
        functools.partial(home_kernel, slot_total),
        in_specs=[pl.BlockSpec(memory_space=pltpu.SMEM)]
        + [pl.BlockSpec(memory_space=pltpu.VMEM)] * 2,
        out_shape=(jax.ShapeDtypeStruct((token_rows, features), jnp.bfloat16), halves, halves),
        scratch_shapes=[pltpu.VMEM((lanes // HSZ, sources * bands, HSZ), jnp.float32)],
        cost_estimate=pl.CostEstimate(flops=1 << 26, bytes_accessed=2 << 20, transcendentals=0),
        name="home",
    )
    home, keep, give = pick_home(core.reshape(1), picks, returned)
    both = jnp.stack([keep, shifted(give, "seq_2", 1)])
    rows = [both] + [shifted(both, "seq_1", k) for k in range(1, cols)]

    homes = [home] + [shifted(home, "head", k) for k in range(1, heads)]

    share = model // cols // depth
    kept, *sent = pl.pallas_call(
        functools.partial(weight_kernel, cols, depth),
        in_specs=[pl.BlockSpec(memory_space=pltpu.SMEM)]
        + [pl.BlockSpec(memory_space=pltpu.VMEM)] * (3 * cols),
        out_shape=[jax.ShapeDtypeStruct((half, share), jnp.float32)]
        + [jax.ShapeDtypeStruct((half, share), jnp.bfloat16)] * (depth - 1),
        scratch_shapes=[pltpu.VMEM((half, model // cols), jnp.float32)],
        cost_estimate=pl.CostEstimate(
            flops=2 * half * model * 2 * token_rows, bytes_accessed=4 << 20, transcendentals=0
        ),
        name="weight",
    )(lax.axis_index("seq_0").reshape(1), *outs, *rows)
    far = sorted(range(1, depth), key=lambda k: abs(2 * k - depth))
    sent = [shifted(sent[k - 1], "seq_0", k) for k in far]
    summed = kept
    for block in sent:
        summed = summed + block.astype(jnp.float32)
    layer_out = pl.pallas_call(
        functools.partial(layer_kernel, heads),
        out_shape=jax.ShapeDtypeStruct((token_rows, width), jnp.bfloat16),
        cost_estimate=pl.CostEstimate(
            flops=2 * token_rows * features * model, bytes_accessed=5 << 20, transcendentals=0
        ),
        name="layer",
    )(*homes, *w_mine)
    low, high = summed[:, : share // 2], summed[:, share // 2 :]
    keep = jnp.where(core == 0, low, high)
    got = shifted(jnp.where(core == 0, high, low), "seq_2", 1)
    grad_weight = jnp.concatenate(
        [jnp.where(core == 0, keep, got), jnp.where(core == 0, got, keep)], axis=0
    )

    back_all = picked(back, returned_grads.reshape(slot_rows, 3 * features))
    grad_queries = back_all[:, :features]
    grad_keys = back_all[:, features : 2 * features]
    grad_values = back_all[:, 2 * features :]
    return (layer_out, grad_queries, grad_keys, grad_values, grad_weight)


def solution(mesh):
    finer = Mesh(
        mesh.devices.reshape(8, 4, 2, mesh.shape["head"]), ("seq_0", "seq_1", "seq_2", "head")
    )
    placed = (P(SEQ, "head"), P(SEQ, "head"), P(SEQ, "head"), P(), P("head", None), P(SEQ, None))
    return jax.shard_map(
        per_device,
        mesh=finer,
        in_specs=placed,
        out_specs=(P(SEQ, "head"), P(SEQ, "head"), P(SEQ, "head"), P(SEQ, "head"), P("head", SEQ)),
        check_vma=False,
    )
```

```python
import functools
import math

import jax
import jax.numpy as jnp
from jax import lax
from jax.experimental import pallas as pl
from jax.experimental.pallas import tpu as pltpu
from jax.sharding import Mesh
from jax.sharding import PartitionSpec as P


HSZ = 128
SEQ = ("seq_0", "seq_1", "seq_2")


def shifted(value, axis, by):
    length = lax.axis_size(axis)
    return lax.ppermute(value, axis, [(i, (i + by) % length) for i in range(length)])


def passed_along(value, axis, by):
    length = lax.axis_size(axis)
    pairs = [(i, i + by) for i in range(length) if 0 <= i + by < length]
    return lax.ppermute(value, axis, pairs)


def member_table(bucket_grid, owner, slot_count):
    sources, stride = bucket_grid.shape
    matches = bucket_grid == owner
    token = jnp.arange(stride)
    earlier = (token[:, None] < token[None, :]).astype(jnp.bfloat16)
    ranking = jnp.dot(matches.astype(jnp.bfloat16), earlier, preferred_element_type=jnp.float32)
    offsets = (
        jnp.arange(sources, dtype=jnp.int32)[:, None] * stride
        + jnp.arange(stride, dtype=jnp.int32)[None, :]
    )
    where_at = []
    present = []
    for slot in range(slot_count):
        placed = (matches & (ranking == slot)).astype(jnp.int32)
        where_at.append(jnp.sum(placed * offsets, axis=1))
        present.append(jnp.sum(placed, axis=1))
    return (jnp.stack(where_at, axis=1).reshape(-1), jnp.stack(present, axis=1).reshape(-1))


NEVER = 1 << 30
NT = (((1,), (1,)), ((), ()))
TN = (((0,), (0,)), ((), ()))


def product(left, right, dims=(((1,), (0,)), ((), ()))):
    return lax.dot_general(left, right, dims, preferred_element_type=jnp.float32)


def hidden(query_at, key_at):
    slots = query_at.shape[0]
    seen = key_at <= query_at
    row = lax.broadcasted_iota(jnp.int32, (slots, 2 * slots), 0)
    column = lax.broadcasted_iota(jnp.int32, (slots, 2 * slots), 1)
    return jnp.where(seen | (row == column), 0.0, -1e30)


def bucket_kernel(
    scaling,
    slot_total,
    rows,
    pairs,
    prev,
    query_at,
    key_at,
    attended,
    grad_query,
    own_terms,
    prev_terms,
    held,
    spread,
):
    features = rows.shape[1] // 2
    heads = features // HSZ
    count, bands = attended.shape[0], attended.shape[1]
    tiles = spread.shape[0]
    bias = hidden(query_at[...], key_at[...])
    spread[...] = jnp.zeros(spread.shape, jnp.float32)
    for head in range(heads):
        def part(ref, index):
            return ref[:, index * features + head * HSZ : index * features + (head + 1) * HSZ]

        query, grad = part(rows, 0), part(rows, 1)
        key = jnp.concatenate([part(pairs, 0), part(prev, 0)], axis=0)
        value = jnp.concatenate([part(pairs, 1), part(prev, 1)], axis=0)
        scores = product(query, key, NT) * scaling + bias
        weights = jnp.exp(scores - jnp.max(scores, axis=1, keepdims=True))
        probs = weights * (1.0 / jnp.sum(weights, axis=1, keepdims=True))
        probs_b = probs.astype(jnp.bfloat16)
        out = product(probs_b, value)
        held[...] = out
        for slot in range(slot_total):
            chunk = slot * heads + head
            spread[chunk % tiles, pl.ds(chunk // tiles, count, stride=bands), :] = held[
                pl.ds(slot, count, stride=slot_total), :
            ]
        out = out.astype(jnp.bfloat16).astype(jnp.float32)
        centre = jnp.sum(out * grad.astype(jnp.float32), axis=1, keepdims=True)
        dscores = (probs * (product(grad, value, NT) - centre)).astype(jnp.bfloat16)
        start, end = head * HSZ, (head + 1) * HSZ
        grad_query[:, start:end] = (product(dscores, key) * scaling).astype(jnp.bfloat16)
        to_key = product(dscores, query, TN) * scaling
        to_value = product(probs_b, grad, TN)
        slots = query.shape[0]
        own_terms[:, start:end] = to_key[:slots]
        own_terms[:, features + start : features + end] = to_value[:slots]
        prev_terms[:, start:end] = to_key[slots:].astype(jnp.bfloat16)
        prev_terms[:, features + start : features + end] = to_value[slots:].astype(jnp.bfloat16)
    for tile in range(tiles):
        attended[:, :, tile * HSZ : (tile + 1) * HSZ] = (
            spread[tile].reshape(count, bands, HSZ).astype(jnp.bfloat16)
        )


def weight_kernel(cols, depth, place, *refs):
    outs = refs[: 2 * cols]
    rows = refs[2 * cols : 3 * cols]
    kept = refs[3 * cols]
    sent = refs[3 * cols + 1 : 3 * cols + depth]
    total = refs[-1]
    columns = total.shape[1]
    step = 256
    for start in range(0, columns, step):
        acc = None
        for k in range(cols):
            for side in range(2):
                term = product(rows[k][side], outs[side * cols + k][:, start : start + step], TN)
                acc = term if acc is None else acc + term
        total[:, start : start + step] = acc
    width = columns // depth
    for k in range(depth):
        at = lax.rem(place[0] + k, depth)
        block = total[:, pl.ds(pl.multiple_of(at * width, width), width)]
        if k == 0:
            kept[...] = block
        else:
            sent[k - 1][...] = block.astype(jnp.bfloat16)


def home_kernel(slot_total, core, picks, returned, home, keep, give, spread):
    count, bands, lanes = returned.shape
    _, features = home.shape
    heads = features // HSZ
    tiles = lanes // HSZ
    used = min(tiles, slot_total * heads)
    for tile in range(used):
        block = returned[:, :, tile * HSZ : (tile + 1) * HSZ]
        spread[tile] = block.astype(jnp.float32).reshape(count * bands, HSZ)
    for head in range(heads):
        total = None
        for slot in range(slot_total):
            chunk = slot * heads + head
            rows = spread[chunk % tiles, pl.ds(chunk // tiles, count, stride=bands), :]
            term = product(picks[slot], rows.astype(jnp.bfloat16))
            total = term if total is None else total + term
        home[:, head * HSZ : (head + 1) * HSZ] = total.astype(jnp.bfloat16)
    half = features // 2
    keep[...] = home[:, pl.ds(pl.multiple_of(core[0] * half, HSZ), half)]
    give[...] = home[:, pl.ds(pl.multiple_of((1 - core[0]) * half, HSZ), half)]


def layer_kernel(count, *refs):
    homes, weights, out = refs[:count], refs[count : 2 * count], refs[-1]
    strip = 256
    for start in range(0, out.shape[1], strip):
        total = None
        for k in range(count):
            term = product(homes[k][...], weights[k][:, start : start + strip])
            total = term if total is None else total + term
        out[:, start : start + strip] = total.astype(jnp.bfloat16)


def pack_kernel(slot_total, device, grid, queries, keys, values, out, weight, packed, total, spread, chosen):
    step = pl.program_id(0)
    term = product(out[...], weight[...], NT)

    @pl.when(step == 0)
    def _():
        total[...] = term

    @pl.when(step > 0)
    def _():
        total[...] += term

    tokens, features = queries.shape
    count, bands = packed.shape[0], packed.shape[1]
    tiles = spread.shape[0]

    def place(index, source):
        rows = product(chosen[...], source)
        for part in range(features // HSZ):
            for slot in range(slot_total):
                chunk = (index // 2 * slot_total + slot) * 2 + index % 2
                chunk = chunk * (features // HSZ) + part
                spread[chunk % tiles, pl.ds(chunk // tiles, count, stride=bands), :] = rows[
                    slot * count : (slot + 1) * count, part * HSZ : (part + 1) * HSZ
                ]

    @pl.when(step == 0)
    def _():
        row = lax.broadcasted_iota(jnp.int32, (tokens, tokens), 0)
        column = lax.broadcasted_iota(jnp.int32, (tokens, tokens), 1)
        mine = grid[pl.ds(device[0], 1), :]
        named = jnp.broadcast_to(mine, (tokens, tokens))
        same = (named == named.T) & (row < column)
        ranking = jnp.sum(same.astype(jnp.int32), axis=0, keepdims=True)
        slot_of = ranking * count + mine
        slots = lax.broadcasted_iota(jnp.int32, (slot_total * count, tokens), 0)
        chosen[...] = jnp.where(slots == slot_of, 1.0, 0.0).astype(jnp.bfloat16)

    for index, source in enumerate((keys, values, queries)):

        @pl.when(step == index)
        def _(index=index, source=source):
            place(index, source[...])

    @pl.when(step == pl.num_programs(0) - 1)
    def _():
        place(3, total[...].astype(jnp.bfloat16))
        for tile in range(tiles):
            packed[:, :, tile * HSZ : (tile + 1) * HSZ] = (
                spread[tile].reshape(count, bands, HSZ).astype(jnp.bfloat16)
            )


def slot_matrix(mine, slot_total, count):
    token = jnp.arange(mine.shape[0])
    same = (mine[:, None] == mine[None, :]) & (token[None, :] < token[:, None])
    ranking = jnp.sum(same.astype(jnp.int32), axis=1)
    owner = jnp.arange(count)[None, :]
    picks = jnp.stack(
        [
            ((mine[:, None] == owner) & (ranking[:, None] == k)).astype(jnp.bfloat16)
            for k in range(slot_total)
        ]
    )
    slot = jnp.arange(count * slot_total)[None, :]
    back = (slot == (mine * slot_total + ranking)[:, None]).astype(jnp.bfloat16)
    return back, picks


def picked(selection, rows):
    return jnp.dot(selection, rows, preferred_element_type=jnp.float32).astype(jnp.bfloat16)


def per_device(queries, keys, values, bucket, w_out, grad_out):
    sources = lax.axis_size(SEQ)
    device = lax.axis_index(SEQ)
    col = lax.axis_index("seq_1")
    core = lax.axis_index("seq_2")
    head = lax.axis_index("head")
    cols = lax.axis_size("seq_1")
    depth = lax.axis_size("seq_0")
    heads = lax.axis_size("head")
    token_rows, features = queries.shape
    model = grad_out.shape[1]
    groups = features // HSZ
    slot_total = max(2, 3 * token_rows // (2 * sources))
    slot_rows = sources * slot_total
    scaling = 1.0 / math.sqrt(HSZ)
    bucket_grid = bucket[:, 0].reshape(sources, token_rows)
    mine = lax.dynamic_index_in_dim(bucket_grid, device, 0, keepdims=False)
    back, picks = slot_matrix(mine, slot_total, sources)
    bands = 8
    split = 4
    whole = pl.BlockSpec((token_rows, features), lambda k: (0, 0))
    packed = pl.pallas_call(
        functools.partial(pack_kernel, slot_total),
        grid=(split,),
        in_specs=[
            pl.BlockSpec(memory_space=pltpu.SMEM),
            pl.BlockSpec((sources, token_rows), lambda k: (0, 0)),
            whole,
            whole,
            whole,
            pl.BlockSpec((token_rows, model // split), lambda k: (0, k)),
            pl.BlockSpec((features, model // split), lambda k: (0, k)),
        ],
        out_specs=pl.BlockSpec(
            (sources, bands, slot_total * 4 * features // bands), lambda k: (0, 0, 0)
        ),
        out_shape=jax.ShapeDtypeStruct(
            (sources, bands, slot_total * 4 * features // bands), jnp.bfloat16
        ),
        scratch_shapes=[
            pltpu.VMEM((token_rows, features), jnp.float32),
            pltpu.VMEM((slot_total * 4 * features // bands // HSZ, sources * bands, HSZ), jnp.float32),
            pltpu.VMEM((slot_rows, token_rows), jnp.bfloat16),
        ],
        cost_estimate=pl.CostEstimate(
            flops=2 * token_rows * features * model, bytes_accessed=6 << 20, transcendentals=0
        ),
        name="pack",
    )(device.reshape(1), bucket_grid, queries, keys, values, grad_out, w_out)
    arrived = lax.all_to_all(packed, SEQ, split_axis=0, concat_axis=0, tiled=True)

    width = model // heads
    w_blocks = [
        lax.dynamic_slice_in_dim(w_out, (head + k) % heads * width, width, axis=1)
        for k in range(heads)
    ]
    w_mine = [
        shifted(w_blocks[k], "head", k) if k in (1, heads - 1) else w_blocks[k]
        for k in range(heads)
    ]

    where_here, alive_here = member_table(bucket_grid, device, slot_total)
    where_before, alive_before = member_table(bucket_grid, device - 1, slot_total)
    query_at = jnp.where(alive_here > 0, where_here, -1)[:, None]
    key_at = jnp.concatenate(
        [
            jnp.where(alive_here > 0, where_here, NEVER),
            jnp.where(alive_before > 0, where_before, NEVER),
        ]
    )[None, :]

    chunks = grad_out.reshape(token_rows, depth, cols, model // (depth * cols))
    out_blocks = jnp.moveaxis(chunks, 2, 0).reshape(cols, token_rows, model // cols)
    outs = [lax.dynamic_index_in_dim(out_blocks, col, 0, keepdims=False)]
    for k in range(1, cols):
        block = lax.dynamic_index_in_dim(out_blocks, (col + k) % cols, 0, keepdims=False)
        outs.append(shifted(block, "seq_1", k))
    arrived, query_at, key_at, back, picks = lax.optimization_barrier(
        (arrived, query_at, key_at, back, picks)
    )
    pair_rows = arrived[:, : bands // 2].reshape(slot_rows, 2 * features)
    prev = passed_along(pair_rows, SEQ, 1)
    arrived, pair_rows = lax.optimization_barrier((arrived, pair_rows))
    query_rows = arrived[:, bands // 2 :].reshape(slot_rows, 2 * features)
    products = 2 * groups * slot_rows * 2 * slot_rows * HSZ
    lanes = -(-slot_total * groups // bands) * HSZ
    pair = (slot_rows, 2 * features)
    attended, grad_query, own_terms, prev_terms = pl.pallas_call(
        functools.partial(bucket_kernel, scaling, slot_total),
        out_shape=(
            jax.ShapeDtypeStruct((sources, bands, lanes), jnp.bfloat16),
            jax.ShapeDtypeStruct((slot_rows, features), jnp.bfloat16),
            jax.ShapeDtypeStruct(pair, jnp.float32),
            jax.ShapeDtypeStruct(pair, jnp.bfloat16),
        ),
        scratch_shapes=[
            pltpu.VMEM((slot_rows, HSZ), jnp.float32),
            pltpu.VMEM((lanes // HSZ, sources * bands, HSZ), jnp.float32),
        ],
        cost_estimate=pl.CostEstimate(
            flops=6 * products, bytes_accessed=3 << 20, transcendentals=0
        ),
        name="bucket",
    )(query_rows, pair_rows, prev, query_at, key_at)
    attended, *moved = lax.optimization_barrier((attended, *w_mine, *outs))
    w_mine, outs = moved[:heads], moved[heads:]
    pair_next = passed_along(prev_terms, SEQ, -1)
    w_mine[2] = shifted(w_mine[2], "head", 2)
    outs = outs + [shifted(block, "seq_2", 1) for block in outs]
    returned = lax.all_to_all(attended, SEQ, split_axis=0, concat_axis=0, tiled=True)
    pair_total = (own_terms + pair_next.astype(jnp.float32)).astype(jnp.bfloat16)
    grads = jnp.concatenate([grad_query, pair_total], axis=1)
    grads = grads.reshape(sources, 4, slot_total * 3 * features // 4)
    returned, *outs = lax.optimization_barrier((returned, *outs))
    returned_grads = lax.all_to_all(grads, SEQ, split_axis=0, concat_axis=0, tiled=True)
    half = features // 2
    halves = jax.ShapeDtypeStruct((token_rows, half), jnp.bfloat16)
    pick_home = pl.pallas_call(
        functools.partial(home_kernel, slot_total),
        in_specs=[pl.BlockSpec(memory_space=pltpu.SMEM)]
        + [pl.BlockSpec(memory_space=pltpu.VMEM)] * 2,
        out_shape=(jax.ShapeDtypeStruct((token_rows, features), jnp.bfloat16), halves, halves),
        scratch_shapes=[pltpu.VMEM((lanes // HSZ, sources * bands, HSZ), jnp.float32)],
        cost_estimate=pl.CostEstimate(flops=1 << 26, bytes_accessed=2 << 20, transcendentals=0),
        name="home",
    )
    home, keep, give = pick_home(core.reshape(1), picks, returned)
    both = jnp.stack([keep, shifted(give, "seq_2", 1)])
    rows = [both] + [shifted(both, "seq_1", k) for k in range(1, cols)]

    homes = [home] + [shifted(home, "head", k) for k in range(1, heads)]

    share = model // cols // depth
    kept, *sent = pl.pallas_call(
        functools.partial(weight_kernel, cols, depth),
        in_specs=[pl.BlockSpec(memory_space=pltpu.SMEM)]
        + [pl.BlockSpec(memory_space=pltpu.VMEM)] * (3 * cols),
        out_shape=[jax.ShapeDtypeStruct((half, share), jnp.float32)]
        + [jax.ShapeDtypeStruct((half, share), jnp.bfloat16)] * (depth - 1),
        scratch_shapes=[pltpu.VMEM((half, model // cols), jnp.float32)],
        cost_estimate=pl.CostEstimate(
            flops=2 * half * model * 2 * token_rows, bytes_accessed=4 << 20, transcendentals=0
        ),
        name="weight",
    )(lax.axis_index("seq_0").reshape(1), *outs, *rows)
    far = sorted(range(1, depth), key=lambda k: abs(2 * k - depth))
    sent = [shifted(sent[k - 1], "seq_0", k) for k in far]
    summed = kept
    for block in sent:
        summed = summed + block.astype(jnp.float32)
    layer_out = pl.pallas_call(
        functools.partial(layer_kernel, heads),
        out_shape=jax.ShapeDtypeStruct((token_rows, width), jnp.bfloat16),
        cost_estimate=pl.CostEstimate(
            flops=2 * token_rows * features * model, bytes_accessed=5 << 20, transcendentals=0
        ),
        name="layer",
    )(*homes, *w_mine)
    low, high = summed[:, : share // 2], summed[:, share // 2 :]
    keep = jnp.where(core == 0, low, high)
    got = shifted(jnp.where(core == 0, high, low), "seq_2", 1)
    grad_weight = jnp.concatenate(
        [jnp.where(core == 0, keep, got), jnp.where(core == 0, got, keep)], axis=0
    )

    back_all = picked(back, returned_grads.reshape(slot_rows, 3 * features))
    grad_queries = back_all[:, :features]
    grad_keys = back_all[:, features : 2 * features]
    grad_values = back_all[:, 2 * features :]
    return (layer_out, grad_queries, grad_keys, grad_values, grad_weight)


def solution(mesh):
    finer = Mesh(
        mesh.devices.reshape(8, 4, 2, mesh.shape["head"]), ("seq_0", "seq_1", "seq_2", "head")
    )
    placed = (P(SEQ, "head"), P(SEQ, "head"), P(SEQ, "head"), P(), P("head", None), P(SEQ, None))
    return jax.shard_map(
        per_device,
        mesh=finer,
        in_specs=placed,
        out_specs=(P(SEQ, "head"), P(SEQ, "head"), P(SEQ, "head"), P(SEQ, "head"), P("head", SEQ)),
        check_vma=False,
    )
```

```python
import functools
import math

import jax
import jax.numpy as jnp
from jax import lax
from jax.experimental import pallas as pl
from jax.experimental.pallas import tpu as pltpu
from jax.sharding import Mesh
from jax.sharding import PartitionSpec as P


HSZ = 128
SEQ = ("seq_0", "seq_1", "seq_2")


def shifted(value, axis, by):
    length = lax.axis_size(axis)
    return lax.ppermute(value, axis, [(i, (i + by) % length) for i in range(length)])


def passed_along(value, axis, by):
    length = lax.axis_size(axis)
    pairs = [(i, i + by) for i in range(length) if 0 <= i + by < length]
    return lax.ppermute(value, axis, pairs)


def member_table(bucket_grid, owner, slot_count):
    sources, stride = bucket_grid.shape
    matches = bucket_grid == owner
    token = jnp.arange(stride)
    earlier = (token[:, None] < token[None, :]).astype(jnp.bfloat16)
    ranking = jnp.dot(matches.astype(jnp.bfloat16), earlier, preferred_element_type=jnp.float32)
    offsets = (
        jnp.arange(sources, dtype=jnp.int32)[:, None] * stride
        + jnp.arange(stride, dtype=jnp.int32)[None, :]
    )
    where_at = []
    present = []
    for slot in range(slot_count):
        placed = (matches & (ranking == slot)).astype(jnp.int32)
        where_at.append(jnp.sum(placed * offsets, axis=1))
        present.append(jnp.sum(placed, axis=1))
    return (jnp.stack(where_at, axis=1).reshape(-1), jnp.stack(present, axis=1).reshape(-1))


NEVER = 1 << 30
NT = (((1,), (1,)), ((), ()))
TN = (((0,), (0,)), ((), ()))


def product(left, right, dims=(((1,), (0,)), ((), ()))):
    return lax.dot_general(left, right, dims, preferred_element_type=jnp.float32)


def hidden(query_at, key_at):
    slots = query_at.shape[0]
    seen = key_at <= query_at
    row = lax.broadcasted_iota(jnp.int32, (slots, 2 * slots), 0)
    column = lax.broadcasted_iota(jnp.int32, (slots, 2 * slots), 1)
    return jnp.where(seen | (row == column), 0.0, -1e30)


def bucket_kernel(
    scaling,
    slot_total,
    rows,
    pairs,
    prev,
    query_at,
    key_at,
    attended,
    grad_query,
    own_terms,
    prev_terms,
    held,
    spread,
):
    features = rows.shape[1] // 2
    heads = features // HSZ
    count, bands = attended.shape[0], attended.shape[1]
    tiles = spread.shape[0]
    bias = hidden(query_at[...], key_at[...])
    spread[...] = jnp.zeros(spread.shape, jnp.float32)
    for head in range(heads):
        def part(ref, index):
            return ref[:, index * features + head * HSZ : index * features + (head + 1) * HSZ]

        query, grad = part(rows, 0), part(rows, 1)
        key = jnp.concatenate([part(pairs, 0), part(prev, 0)], axis=0)
        value = jnp.concatenate([part(pairs, 1), part(prev, 1)], axis=0)
        scores = product(query, key, NT) * scaling + bias
        weights = jnp.exp(scores - jnp.max(scores, axis=1, keepdims=True))
        probs = weights * (1.0 / jnp.sum(weights, axis=1, keepdims=True))
        probs_b = probs.astype(jnp.bfloat16)
        out = product(probs_b, value)
        held[...] = out
        for slot in range(slot_total):
            chunk = slot * heads + head
            spread[chunk % tiles, pl.ds(chunk // tiles, count, stride=bands), :] = held[
                pl.ds(slot, count, stride=slot_total), :
            ]
        out = out.astype(jnp.bfloat16).astype(jnp.float32)
        centre = jnp.sum(out * grad.astype(jnp.float32), axis=1, keepdims=True)
        dscores = (probs * (product(grad, value, NT) - centre)).astype(jnp.bfloat16)
        start, end = head * HSZ, (head + 1) * HSZ
        grad_query[:, start:end] = (product(dscores, key) * scaling).astype(jnp.bfloat16)
        to_key = product(dscores, query, TN) * scaling
        to_value = product(probs_b, grad, TN)
        slots = query.shape[0]
        own_terms[:, start:end] = to_key[:slots]
        own_terms[:, features + start : features + end] = to_value[:slots]
        prev_terms[:, start:end] = to_key[slots:].astype(jnp.bfloat16)
        prev_terms[:, features + start : features + end] = to_value[slots:].astype(jnp.bfloat16)
    for tile in range(tiles):
        attended[:, :, tile * HSZ : (tile + 1) * HSZ] = (
            spread[tile].reshape(count, bands, HSZ).astype(jnp.bfloat16)
        )


def weight_kernel(cols, depth, place, *refs):
    outs = refs[: 2 * cols]
    rows = refs[2 * cols : 3 * cols]
    kept = refs[3 * cols]
    sent = refs[3 * cols + 1 : 3 * cols + depth]
    total = refs[-1]
    columns = total.shape[1]
    step = 256
    for start in range(0, columns, step):
        acc = None
        for k in range(cols):
            for side in range(2):
                term = product(rows[k][side], outs[side * cols + k][:, start : start + step], TN)
                acc = term if acc is None else acc + term
        total[:, start : start + step] = acc
    width = columns // depth
    for k in range(depth):
        at = lax.rem(place[0] + k, depth)
        block = total[:, pl.ds(pl.multiple_of(at * width, width), width)]
        if k == 0:
            kept[...] = block
        else:
            sent[k - 1][...] = block.astype(jnp.bfloat16)


def home_kernel(slot_total, core, picks, returned, home, keep, give, spread):
    count, bands, lanes = returned.shape
    _, features = home.shape
    heads = features // HSZ
    tiles = lanes // HSZ
    used = min(tiles, slot_total * heads)
    for tile in range(used):
        block = returned[:, :, tile * HSZ : (tile + 1) * HSZ]
        spread[tile] = block.astype(jnp.float32).reshape(count * bands, HSZ)
    for head in range(heads):
        total = None
        for slot in range(slot_total):
            chunk = slot * heads + head
            rows = spread[chunk % tiles, pl.ds(chunk // tiles, count, stride=bands), :]
            term = product(picks[slot], rows.astype(jnp.bfloat16))
            total = term if total is None else total + term
        home[:, head * HSZ : (head + 1) * HSZ] = total.astype(jnp.bfloat16)
    half = features // 2
    keep[...] = home[:, pl.ds(pl.multiple_of(core[0] * half, HSZ), half)]
    give[...] = home[:, pl.ds(pl.multiple_of((1 - core[0]) * half, HSZ), half)]


def layer_kernel(count, *refs):
    homes, weights, out = refs[:count], refs[count : 2 * count], refs[-1]
    strip = 256
    for start in range(0, out.shape[1], strip):
        total = None
        for k in range(count):
            term = product(homes[k][...], weights[k][:, start : start + strip])
            total = term if total is None else total + term
        out[:, start : start + strip] = total.astype(jnp.bfloat16)


def pack_kernel(slot_total, device, grid, queries, keys, values, out, weight, packed, total, spread, chosen):
    step = pl.program_id(0)
    term = product(out[...], weight[...], NT)

    @pl.when(step == 0)
    def _():
        total[...] = term

    @pl.when(step > 0)
    def _():
        total[...] += term

    tokens, features = queries.shape
    count, bands = packed.shape[0], packed.shape[1]
    tiles = spread.shape[0]

    def place(index, source):
        rows = product(chosen[...], source)
        for part in range(features // HSZ):
            for slot in range(slot_total):
                chunk = (index // 2 * slot_total + slot) * 2 + index % 2
                chunk = chunk * (features // HSZ) + part
                spread[chunk % tiles, pl.ds(chunk // tiles, count, stride=bands), :] = rows[
                    slot * count : (slot + 1) * count, part * HSZ : (part + 1) * HSZ
                ]

    @pl.when(step == 0)
    def _():
        row = lax.broadcasted_iota(jnp.int32, (tokens, tokens), 0)
        column = lax.broadcasted_iota(jnp.int32, (tokens, tokens), 1)
        mine = grid[pl.ds(device[0], 1), :]
        named = jnp.broadcast_to(mine, (tokens, tokens))
        same = (named == named.T) & (row < column)
        ranking = jnp.sum(same.astype(jnp.int32), axis=0, keepdims=True)
        slot_of = ranking * count + mine
        slots = lax.broadcasted_iota(jnp.int32, (slot_total * count, tokens), 0)
        chosen[...] = jnp.where(slots == slot_of, 1.0, 0.0).astype(jnp.bfloat16)

    for index, source in enumerate((keys, values, queries)):

        @pl.when(step == index)
        def _(index=index, source=source):
            place(index, source[...])

    @pl.when(step == pl.num_programs(0) - 1)
    def _():
        place(3, total[...].astype(jnp.bfloat16))
        for tile in range(tiles):
            packed[:, :, tile * HSZ : (tile + 1) * HSZ] = (
                spread[tile].reshape(count, bands, HSZ).astype(jnp.bfloat16)
            )


def slot_matrix(mine, slot_total, count):
    token = jnp.arange(mine.shape[0])
    same = (mine[:, None] == mine[None, :]) & (token[None, :] < token[:, None])
    ranking = jnp.sum(same.astype(jnp.int32), axis=1)
    owner = jnp.arange(count)[None, :]
    picks = jnp.stack(
        [
            ((mine[:, None] == owner) & (ranking[:, None] == k)).astype(jnp.bfloat16)
            for k in range(slot_total)
        ]
    )
    slot = jnp.arange(count * slot_total)[None, :]
    back = (slot == (mine * slot_total + ranking)[:, None]).astype(jnp.bfloat16)
    return back, picks


def picked(selection, rows):
    return jnp.dot(selection, rows, preferred_element_type=jnp.float32).astype(jnp.bfloat16)


def per_device(queries, keys, values, bucket, w_out, grad_out):
    sources = lax.axis_size(SEQ)
    device = lax.axis_index(SEQ)
    col = lax.axis_index("seq_1")
    core = lax.axis_index("seq_2")
    head = lax.axis_index("head")
    cols = lax.axis_size("seq_1")
    depth = lax.axis_size("seq_0")
    heads = lax.axis_size("head")
    token_rows, features = queries.shape
    model = grad_out.shape[1]
    groups = features // HSZ
    slot_total = max(2, 3 * token_rows // (2 * sources))
    slot_rows = sources * slot_total
    scaling = 1.0 / math.sqrt(HSZ)
    bucket_grid = bucket[:, 0].reshape(sources, token_rows)
    mine = lax.dynamic_index_in_dim(bucket_grid, device, 0, keepdims=False)
    back, picks = slot_matrix(mine, slot_total, sources)
    bands = 8
    split = 4
    whole = pl.BlockSpec((token_rows, features), lambda k: (0, 0))
    packed = pl.pallas_call(
        functools.partial(pack_kernel, slot_total),
        grid=(split,),
        in_specs=[
            pl.BlockSpec(memory_space=pltpu.SMEM),
            pl.BlockSpec((sources, token_rows), lambda k: (0, 0)),
            whole,
            whole,
            whole,
            pl.BlockSpec((token_rows, model // split), lambda k: (0, k)),
            pl.BlockSpec((features, model // split), lambda k: (0, k)),
        ],
        out_specs=pl.BlockSpec(
            (sources, bands, slot_total * 4 * features // bands), lambda k: (0, 0, 0)
        ),
        out_shape=jax.ShapeDtypeStruct(
            (sources, bands, slot_total * 4 * features // bands), jnp.bfloat16
        ),
        scratch_shapes=[
            pltpu.VMEM((token_rows, features), jnp.float32),
            pltpu.VMEM((slot_total * 4 * features // bands // HSZ, sources * bands, HSZ), jnp.float32),
            pltpu.VMEM((slot_rows, token_rows), jnp.bfloat16),
        ],
        cost_estimate=pl.CostEstimate(
            flops=2 * token_rows * features * model, bytes_accessed=6 << 20, transcendentals=0
        ),
        name="pack",
    )(device.reshape(1), bucket_grid, queries, keys, values, grad_out, w_out)
    arrived = lax.all_to_all(packed, SEQ, split_axis=0, concat_axis=0, tiled=True)

    width = model // heads
    w_blocks = [
        lax.dynamic_slice_in_dim(w_out, (head + k) % heads * width, width, axis=1)
        for k in range(heads)
    ]
    w_mine = [
        shifted(w_blocks[k], "head", k) if k in (1, heads - 1) else w_blocks[k]
        for k in range(heads)
    ]

    where_here, alive_here = member_table(bucket_grid, device, slot_total)
    where_before, alive_before = member_table(bucket_grid, device - 1, slot_total)
    query_at = jnp.where(alive_here > 0, where_here, -1)[:, None]
    key_at = jnp.concatenate(
        [
            jnp.where(alive_here > 0, where_here, NEVER),
            jnp.where(alive_before > 0, where_before, NEVER),
        ]
    )[None, :]

    chunks = grad_out.reshape(token_rows, depth, cols, model // (depth * cols))
    out_blocks = jnp.moveaxis(chunks, 2, 0).reshape(cols, token_rows, model // cols)
    outs = [lax.dynamic_index_in_dim(out_blocks, col, 0, keepdims=False)]
    for k in range(1, cols):
        block = lax.dynamic_index_in_dim(out_blocks, (col + k) % cols, 0, keepdims=False)
        outs.append(shifted(block, "seq_1", k))
    arrived, query_at, key_at, back, picks = lax.optimization_barrier(
        (arrived, query_at, key_at, back, picks)
    )
    pair_rows = arrived[:, : bands // 2].reshape(slot_rows, 2 * features)
    prev = passed_along(pair_rows, SEQ, 1)
    arrived, pair_rows = lax.optimization_barrier((arrived, pair_rows))
    query_rows = arrived[:, bands // 2 :].reshape(slot_rows, 2 * features)
    products = 2 * groups * slot_rows * 2 * slot_rows * HSZ
    lanes = -(-slot_total * groups // bands) * HSZ
    pair = (slot_rows, 2 * features)
    attended, grad_query, own_terms, prev_terms = pl.pallas_call(
        functools.partial(bucket_kernel, scaling, slot_total),
        out_shape=(
            jax.ShapeDtypeStruct((sources, bands, lanes), jnp.bfloat16),
            jax.ShapeDtypeStruct((slot_rows, features), jnp.bfloat16),
            jax.ShapeDtypeStruct(pair, jnp.float32),
            jax.ShapeDtypeStruct(pair, jnp.bfloat16),
        ),
        scratch_shapes=[
            pltpu.VMEM((slot_rows, HSZ), jnp.float32),
            pltpu.VMEM((lanes // HSZ, sources * bands, HSZ), jnp.float32),
        ],
        cost_estimate=pl.CostEstimate(
            flops=6 * products, bytes_accessed=3 << 20, transcendentals=0
        ),
        name="bucket",
    )(query_rows, pair_rows, prev, query_at, key_at)
    attended, w_mine[1], w_mine[-1], *outs[1:] = lax.optimization_barrier(
        (attended, w_mine[1], w_mine[-1], *outs[1:])
    )
    pair_next = passed_along(prev_terms, SEQ, -1)
    w_mine[2] = shifted(w_mine[2], "head", 2)
    outs = outs + [shifted(block, "seq_2", 1) for block in outs]
    returned = lax.all_to_all(attended, SEQ, split_axis=0, concat_axis=0, tiled=True)
    pair_total = (own_terms + pair_next.astype(jnp.float32)).astype(jnp.bfloat16)
    grads = jnp.concatenate([grad_query, pair_total], axis=1)
    grads = grads.reshape(sources, 4, slot_total * 3 * features // 4)
    returned, *outs = lax.optimization_barrier((returned, *outs))
    returned_grads = lax.all_to_all(grads, SEQ, split_axis=0, concat_axis=0, tiled=True)
    half = features // 2
    halves = jax.ShapeDtypeStruct((token_rows, half), jnp.bfloat16)
    pick_home = pl.pallas_call(
        functools.partial(home_kernel, slot_total),
        in_specs=[pl.BlockSpec(memory_space=pltpu.SMEM)]
        + [pl.BlockSpec(memory_space=pltpu.VMEM)] * 2,
        out_shape=(jax.ShapeDtypeStruct((token_rows, features), jnp.bfloat16), halves, halves),
        scratch_shapes=[pltpu.VMEM((lanes // HSZ, sources * bands, HSZ), jnp.float32)],
        cost_estimate=pl.CostEstimate(flops=1 << 26, bytes_accessed=2 << 20, transcendentals=0),
        name="home",
    )
    home, keep, give = pick_home(core.reshape(1), picks, returned)
    got = shifted(give, "seq_2", 1)
    both = jnp.stack([keep, got])
    rows = [both] + [shifted(both, "seq_1", k) for k in range(1, cols)]

    homes = [home] + [shifted(home, "head", k) for k in range(1, heads)]

    share = model // cols // depth
    kept, *sent = pl.pallas_call(
        functools.partial(weight_kernel, cols, depth),
        in_specs=[pl.BlockSpec(memory_space=pltpu.SMEM)]
        + [pl.BlockSpec(memory_space=pltpu.VMEM)] * (3 * cols),
        out_shape=[jax.ShapeDtypeStruct((half, share), jnp.float32)]
        + [jax.ShapeDtypeStruct((half, share), jnp.bfloat16)] * (depth - 1),
        scratch_shapes=[pltpu.VMEM((half, model // cols), jnp.float32)],
        cost_estimate=pl.CostEstimate(
            flops=2 * half * model * 2 * token_rows, bytes_accessed=4 << 20, transcendentals=0
        ),
        name="weight",
    )(lax.axis_index("seq_0").reshape(1), *outs, *rows)
    far = sorted(range(1, depth), key=lambda k: abs(2 * k - depth))
    sent = [shifted(sent[k - 1], "seq_0", k) for k in far]
    summed = kept
    for block in sent:
        summed = summed + block.astype(jnp.float32)
    layer_out = pl.pallas_call(
        functools.partial(layer_kernel, heads),
        out_shape=jax.ShapeDtypeStruct((token_rows, width), jnp.bfloat16),
        cost_estimate=pl.CostEstimate(
            flops=2 * token_rows * features * model, bytes_accessed=5 << 20, transcendentals=0
        ),
        name="layer",
    )(*homes, *w_mine)
    low, high = summed[:, : share // 2], summed[:, share // 2 :]
    keep = jnp.where(core == 0, low, high)
    got = shifted(jnp.where(core == 0, high, low), "seq_2", 1)
    grad_weight = jnp.concatenate(
        [jnp.where(core == 0, keep, got), jnp.where(core == 0, got, keep)], axis=0
    )

    back_all = picked(back, returned_grads.reshape(slot_rows, 3 * features))
    grad_queries = back_all[:, :features]
    grad_keys = back_all[:, features : 2 * features]
    grad_values = back_all[:, 2 * features :]
    return (layer_out, grad_queries, grad_keys, grad_values, grad_weight)


def solution(mesh):
    finer = Mesh(
        mesh.devices.reshape(8, 4, 2, mesh.shape["head"]), ("seq_0", "seq_1", "seq_2", "head")
    )
    placed = (P(SEQ, "head"), P(SEQ, "head"), P(SEQ, "head"), P(), P("head", None), P(SEQ, None))
    return jax.shard_map(
        per_device,
        mesh=finer,
        in_specs=placed,
        out_specs=(P(SEQ, "head"), P(SEQ, "head"), P(SEQ, "head"), P(SEQ, "head"), P("head", SEQ)),
        check_vma=False,
    )
```
